32 devices in a mesh: gz: 16 (over z, y, core), ta: 2 (over x).
Axes of the slice: x: 2, y: 2, z: 4, core: 2. Of those that a mesh axis runs over, the one named last changes fastest.
Arguments:
- outputs_fwd: bfloat16 [4, 32, 64, 1280], P('ta', 'gz'), may hold values from -6 to 6
- cotangent: bfloat16 [4, 32, 64, 1280], P('ta', 'gz'), may hold values from -6 to 6
- spatial_weight: bfloat16 [3, 64, 288], replicated, may hold values from -0.21875 to 0.21875
- hidden_bias: float32 [64], replicated, may hold values from -1 to 1
- temporal_weight: bfloat16 [3, 32, 64], replicated, may hold values from -0.4375 to 0.4375
Outputs:
- rebuilt: bfloat16 [4, 32, 32, 1280], P('ta', 'gz')
- grad_in: bfloat16 [4, 32, 32, 1280], P('ta', 'gz')
- grad_spatial: float32 [3, 64, 288], replicated
- grad_bias: float32 [64], replicated
- grad_temporal: float32 [3, 32, 64], replicated
The draws below stay inside these ranges and needn't reach their ends.
All inputs are finite; a program needn't handle non-finite values.
Results may differ from the reference program's by a relative error of at most 0.0075.
Values may be sent and summed in bfloat16 or wider, within the bound.
A program may use at most 64 MiB of HBM per device.

```python
import math
import jax
import jax.numpy as jnp
from jax import lax

CH = 32
HID = 64
ROWS = 8
COLS = 160
NZ = 32
FRAMES = 4


def level_of(stream_key, dims, split, smallest, high):
    def one(axis_at, parts):
        heights = jax.random.uniform(jax.random.fold_in(jax.random.fold_in(stream_key, 6), axis_at), (parts,), jnp.float32, smallest / len(split), high / len(split))
        return jnp.repeat(jnp.exp(heights), dims[axis_at] // parts).reshape((-1,) + (1,) * (len(dims) - axis_at - 1))

    gain = one(*split[0])
    for cut in split[1:]:
        gain = gain * one(*cut)
    return gain


def bell_draw(stream_key, dims, scale, bound, split=(), kind=jnp.bfloat16):
    drawn = jax.random.normal(stream_key, dims, jnp.float32) * scale
    if len(split) > 0:
        drawn = level_of(stream_key, dims, split, -0.22, 0.18) * drawn
    return jnp.clip(drawn, min=-bound, max=bound).astype(kind)


def setup_inputs(seed: int = 0) -> dict:
    splits = jax.random.split(jax.random.key(seed), 6)
    return {
        "outputs_fwd": bell_draw(splits[0], (FRAMES, NZ, 2 * CH, ROWS * COLS), 1.0, 6.0, ((0, 2), (1, 16))),
        "cotangent": bell_draw(splits[1], (FRAMES, NZ, 2 * CH, ROWS * COLS), 1.0, 6.0, ((0, 2), (1, 16))),
        "spatial_weight": bell_draw(splits[2], (3, HID, 9 * CH), (27 * CH) ** -0.5, 0.21875),
        "hidden_bias": jnp.clip(jax.random.uniform(splits[3], (HID,), jnp.float32, -1.0, 1.0), -1.0, 1.0),
        "temporal_weight": bell_draw(splits[4], (3, CH, HID), (3 * HID) ** -0.5, 0.4375),
    }


def unfold(field):
    leading = field.shape[:-1]
    planar = field.reshape(leading + (ROWS, COLS))
    padded = jnp.pad(planar, [(0, 0)] * len(leading) + [(1, 1), (1, 1)])
    windows = [padded[..., row_off:row_off + ROWS, col_off:col_off + COLS] for row_off in range(3) for col_off in range(3)]
    stacked = jnp.stack(windows, axis=-4)
    return stacked.reshape(leading[:-1] + (9 * leading[-1], ROWS * COLS))

def linear_frame(frame_in, spatial_weight):
    columns = jnp.pad(unfold(frame_in), ((1, 1), (0, 0), (0, 0))).astype(jnp.float32)
    weight = spatial_weight.astype(jnp.float32)
    total = jnp.einsum('oi,zir->zor', weight[0], columns[0:NZ], precision=lax.Precision.HIGHEST)
    total = total + jnp.einsum('oi,zir->zor', weight[1], columns[1:NZ + 1], precision=lax.Precision.HIGHEST)
    total = total + jnp.einsum('oi,zir->zor', weight[2], columns[2:NZ + 2], precision=lax.Precision.HIGHEST)
    return total

def reference(outputs_fwd, cotangent, spatial_weight, hidden_bias, temporal_weight):
    front_half = outputs_fwd[:, :, :CH]
    back_half = outputs_fwd[:, :, CH:]
    grad_front = cotangent[:, :, :CH]
    grad_back = cotangent[:, :, CH:]
    bias_col = hidden_bias.astype(jnp.float32)[None, :, None]

    def activate(frame_in):
        return jax.nn.silu(linear_frame(frame_in, spatial_weight) + bias_col).astype(jnp.bfloat16)
    active = lax.map(activate, front_half)
    tweight = temporal_weight.astype(jnp.float32)

    def frame_step(carry, index):
        spatial_acc, bias_acc, temporal_acc = carry
        near = [active[(index + offset - 1) % FRAMES].astype(jnp.float32) for offset in range(3)]
        mapped = jnp.einsum('oi,zir->zor', tweight[0], near[0], precision=lax.Precision.HIGHEST)
        mapped = mapped + jnp.einsum('oi,zir->zor', tweight[1], near[1], precision=lax.Precision.HIGHEST)
        mapped = mapped + jnp.einsum('oi,zir->zor', tweight[2], near[2], precision=lax.Precision.HIGHEST)
        rebuilt = (back_half[index].astype(jnp.float32) - mapped).astype(jnp.bfloat16)
        grads_near = [grad_back[(index + 1 - offset) % FRAMES].astype(jnp.float32) for offset in range(3)]
        through = jnp.einsum('oi,zor->zir', tweight[0], grads_near[0], precision=lax.Precision.HIGHEST)
        through = through + jnp.einsum('oi,zor->zir', tweight[1], grads_near[1], precision=lax.Precision.HIGHEST)
        through = through + jnp.einsum('oi,zor->zir', tweight[2], grads_near[2], precision=lax.Precision.HIGHEST)
        own_grad = grad_back[index].astype(jnp.float32)
        temporal_acc = temporal_acc + jnp.stack([jnp.einsum('zor,zir->oi', own_grad, near[offset], precision=lax.Precision.HIGHEST) for offset in range(3)])
        frame_in = front_half[index]
        linear_val, pullback = jax.vjp(lambda field: linear_frame(field, spatial_weight), frame_in.astype(jnp.float32))
        hidden_in = linear_val + bias_col
        sigmoid_val = jax.nn.sigmoid(hidden_in)
        hidden_grad = (through * sigmoid_val * (1.0 + hidden_in * (1.0 - sigmoid_val))).astype(jnp.bfloat16)
        grad_value = hidden_grad.astype(jnp.float32)
        columns = jnp.pad(unfold(frame_in), ((1, 1), (0, 0), (0, 0))).astype(jnp.float32)
        spatial_acc = spatial_acc + jnp.stack([jnp.einsum('zor,zir->oi', grad_value, columns[depth:depth + NZ], precision=lax.Precision.HIGHEST) for depth in range(3)])
        bias_acc = bias_acc + lax.optimization_barrier(jnp.sum(grad_value, axis=(0, 2)))
        input_grad = pullback(grad_value)[0]
        grad_in = (grad_front[index].astype(jnp.float32) + input_grad).astype(jnp.bfloat16)
        return ((spatial_acc, bias_acc, temporal_acc), (rebuilt, grad_in))
    start = (jnp.zeros(spatial_weight.shape, jnp.float32), jnp.zeros((HID,), jnp.float32), jnp.zeros(temporal_weight.shape, jnp.float32))
    carry, (rebuilt, grad_in) = lax.scan(frame_step, start, jnp.arange(FRAMES, dtype=jnp.int32))
    factor = 1.0 / math.sqrt(FRAMES * NZ * ROWS * COLS)
    return (rebuilt, grad_in, carry[0] * factor, carry[1] * factor, carry[2] * factor)
```

```python
import functools
import math

import jax
import jax.numpy as jnp
from jax import lax
from jax.experimental import pallas as pl
from jax.experimental.pallas import tpu as pltpu
from jax.sharding import PartitionSpec as P

ROWS = 8
COLS = 160
LANES = 128
F32 = jnp.float32
BF16 = jnp.bfloat16


def groups_of(gz_count, ta_count):
    bits = lambda count: [1 << i for i in range(count.bit_length() - 1)]
    gz_bits = [("gz", bit) for bit in bits(gz_count)]
    ta_bits = [("ta", bit) for bit in bits(ta_count)]
    return gz_bits[:3], gz_bits[3:] + ta_bits


def sum_layout(half, near_count):
    temporal = -(-27 * half // LANES)
    tiles = temporal + -(-(3 * half + 1) // LANES)
    return temporal, -(-tiles // near_count) * near_count


def nn(lhs, rhs):
    return lax.dot_general(lhs, rhs, (((1,), (0,)), ((), ())), preferred_element_type=F32)


def nt(lhs, rhs):
    return lax.dot_general(lhs, rhs, (((1,), (1,)), ((), ())), preferred_element_type=F32)


def tn(lhs, rhs):
    return lax.dot_general(lhs, rhs, (((0,), (0,)), ((), ())), preferred_element_type=F32)


def kernel(
    gz_count, ta_count,
    x_hbm, g_hbm, sw_hbm, bias_hbm, tw_hbm,
    rebuilt_ref, gin_ref, fin,
    cols, hcols, g3, yh, slope, act, parts, mown, msend, mrecv, psend, precv,
    y_ref, y2_ref, g1_ref, sw_ref, bias_ref, tw_ref, wcat, flip, acc, accb, first, second,
    lsem, ysem, g3sem,
    ysem_s, ysem_r, gsem_s, gsem_r, msem_s, msem_r, psem_s, psem_r,
    asem_s, asem_r, bsem_s, bsem_r, csem_s, csem_r,
):
    frames, planes, half, pix = y_ref.shape
    hid = bias_ref.shape[1]
    window = 9 * half
    me_g = lax.axis_index("gz")
    me_t = lax.axis_index("ta")
    has_l = me_g > 0
    has_r = me_g < gz_count - 1
    mesh_id = pl.DeviceIdType.MESH
    ta_r = lax.rem(me_t + 1, ta_count)
    ta_l = lax.rem(me_t + ta_count - 1, ta_count)
    near_bits, far_bits = groups_of(gz_count, ta_count)

    def member(group, flip_mask):
        place = {"gz": me_g, "ta": me_t}
        index = 0
        for order, (axis, bit) in enumerate(group):
            at = me_g if axis == "gz" else me_t
            has = lax.rem(at // bit, 2)
            if flip_mask >> order & 1:
                place[axis] = place[axis] + bit - 2 * bit * has
                has = 1 - has
            index = index + (has << order)
        return (place["gz"], place["ta"]), index

    near_count, far_count = 1 << len(near_bits), 1 << len(far_bits)
    barrier = pltpu.get_barrier_semaphore()

    def greet(dev):
        pl.semaphore_signal(barrier, inc=1, device_id=dev, device_id_type=mesh_id)

    greet((me_g, ta_r))
    greet((me_g, ta_l))

    @pl.when(has_l)
    def _():
        greet((me_g - 1, me_t))

    @pl.when(has_r)
    def _():
        greet((me_g + 1, me_t))

    for j in range(1, near_count):
        greet(member(near_bits, j)[0])
    for j in range(1, far_count):
        greet(member(far_bits, j)[0])

    pairs = (
        (sw_hbm, sw_ref), (tw_hbm, tw_ref), (bias_hbm, bias_ref),
        (x_hbm.at[:, :, half : 2 * half], y2_ref), (g_hbm.at[:, :, 0:half], g1_ref),
    )
    loads = [pltpu.make_async_copy(src, dst, lsem.at[i]) for i, (src, dst) in enumerate(pairs)]
    own = [pltpu.make_async_copy(x_hbm.at[t, :, 0:half], y_ref.at[t], ysem.at[t]) for t in range(frames)]
    local = [
        (s, k, pltpu.make_async_copy(
            g_hbm.at[s + 1 - k, :, half : 2 * half], g3.at[s, :, k * half : (k + 1) * half], g3sem.at[s, k]
        ))
        for s in range(frames) for k in range(3) if 0 <= s + 1 - k < frames
    ]
    for load in own + loads[:3]:
        load.start()
    beside = has_l.astype(jnp.int32) + has_r.astype(jnp.int32)
    pl.semaphore_wait(barrier, near_count + far_count + beside)

    def remote(src, dst, ssem, rsem, dev):
        return pltpu.make_async_remote_copy(
            src_ref=src, dst_ref=dst, send_sem=ssem, recv_sem=rsem, device_id=dev, device_id_type=mesh_id
        )

    y_right = [
        remote(x_hbm.at[t, planes - 1, 0:half], yh.at[0, t], ysem_s.at[0, t], ysem_r.at[0, t], (me_g + 1, me_t))
        for t in range(frames)
    ]
    y_left = [
        remote(x_hbm.at[t, 0, 0:half], yh.at[1, t], ysem_s.at[1, t], ysem_r.at[1, t], (me_g - 1, me_t))
        for t in range(frames)
    ]
    g_left = [
        remote(
            g_hbm.at[0, z, half : 2 * half], g3.at[frames - 1, z, 0:half],
            gsem_s.at[0, z], gsem_r.at[0, z], (me_g, ta_l),
        )
        for z in range(planes)
    ]
    g_right = [
        remote(
            g_hbm.at[frames - 1, z, half : 2 * half], g3.at[0, z, 2 * half : 3 * half],
            gsem_s.at[1, z], gsem_r.at[1, z], (me_g, ta_r),
        )
        for z in range(planes)
    ]
    g_right[0].start()
    for t in range(frames):
        pl.when(has_r)(y_right[t].start)
        pl.when(has_l)(y_left[t].start)
    g_left[0].start()
    for z in range(1, planes):
        g_right[z].start()
        g_left[z].start()
    for _, _, load in local:
        load.start()
    for load in loads[3:]:
        load.start()

    for load in loads[:3]:
        load.wait()
    for dz in range(3):
        wcat[:, dz * window : (dz + 1) * window] = sw_ref[dz]
        turned = sw_ref[dz].astype(F32).T.astype(BF16)
        for w in range(9):
            flip[dz * half : (dz + 1) * half, w * hid : (w + 1) * hid] = turned[(8 - w) * half : (9 - w) * half]
    bias = jnp.broadcast_to(bias_ref[...], (8, hid)).T[:, 0:1]

    place = lax.broadcasted_iota(jnp.int32, (1, pix), 1)
    column = lax.rem(place, COLS)
    col_ok = {-1: column < COLS - 1, 1: column > 0}
    edge = -(-COLS // LANES) * LANES
    zero = jnp.zeros((), BF16)
    head_ok = place[:, 0:edge] >= COLS
    tail_ok = place[:, pix - edge : pix] < pix - COLS

    def unfold(value, out, base):
        rows = value.shape[0]
        for c in (-1, 0, 1):
            source = value if c == 0 else jnp.where(col_ok[c], value, zero)
            for r in (-1, 0, 1):
                shift = (-(r * COLS + c)) % pix
                moved = pltpu.roll(source, shift, 1) if shift else source
                at = pl.ds(base + (3 * (r + 1) + c + 1) * rows, rows)
                if r == -1:
                    out[at, 0:edge] = jnp.where(head_ok, moved[:, 0:edge], zero)
                    out[at, edge:pix] = moved[:, edge:pix]
                elif r == 1:
                    out[at, 0 : pix - edge] = moved[:, 0 : pix - edge]
                    out[at, pix - edge : pix] = jnp.where(tail_ok, moved[:, pix - edge : pix], zero)
                else:
                    out[at, :] = moved

    for t in range(frames):
        own[t].wait()
        for z in range(planes):
            unfold(y_ref[t, z], cols.at[t], (z + 1) * window)

    whole = wcat[...]
    tw = tw_ref[...]
    m_right = [
        remote(msend.at[0, z], mrecv.at[0, z], msem_s.at[0, z], msem_r.at[0, z], (me_g, ta_r)) for z in range(planes)
    ]
    m_left = [
        remote(msend.at[1, z], mrecv.at[1, z], msem_s.at[1, z], msem_r.at[1, z], (me_g, ta_l)) for z in range(planes)
    ]
    last = (planes + 1) * window
    for t in range(frames):

        @pl.when(has_l)
        def _():
            y_right[t].wait_recv()
            unfold(yh[0, t], cols.at[t], 0)

        @pl.when(jnp.logical_not(has_l))
        def _():
            cols[t, 0:window, :] = jnp.zeros((window, pix), BF16)

        @pl.when(has_r)
        def _():
            y_left[t].wait_recv()
            unfold(yh[1, t], cols.at[t], last)

        @pl.when(jnp.logical_not(has_r))
        def _():
            cols[t, last : last + window, :] = jnp.zeros((window, pix), BF16)

        for z in range(planes):
            pre = nn(whole, cols[t, z * window : (z + 3) * window, :]) + bias
            sig = jax.nn.sigmoid(pre)
            active = (pre * sig).astype(BF16)
            slope[t, z] = sig * (1.0 + pre * (1.0 - sig))
            act[t, z] = active
            mapped = nn(tw, active)
            mown[t, z] = mapped
            if t == 0:
                msend[1, z] = mapped[2 * half : 3 * half, :].astype(BF16)
                m_left[z].start()
            if t == frames - 1:
                msend[0, z] = mapped[0:half, :].astype(BF16)
                m_right[z].start()

    for _, _, load in local:
        load.wait()

    temporal = sum_layout(half, near_count)[0]
    tiles = acc.shape[0]
    per = tiles // near_count

    def span(index):
        return pl.ds(index * per, per)

    near_me = member(near_bits, 0)[1]
    far_me = member(far_bits, 0)[1]
    scatter, share, gather = [], [], []
    for j in reversed(range(1, near_count)):
        dev, index = member(near_bits, j)
        scatter.append((j, remote(accb.at[span(index)], first.at[j - 1], asem_s.at[j - 1], asem_r.at[j - 1], dev)))
        mine = fin.at[span(near_me)]
        gather.append(remote(mine, mine, csem_s.at[j - 1], csem_r.at[j - 1], dev))
    for j in reversed(range(1, far_count)):
        dev, _ = member(far_bits, j)
        share.append(remote(second.at[far_me], second.at[far_me], bsem_s.at[j - 1], bsem_r.at[j - 1], dev))

    back = flip[...]

    def p_right(t):
        return remote(psend.at[0, t], precv.at[0, t], psem_s.at[0, t], psem_r.at[0, t], (me_g + 1, me_t))

    def p_left(t):
        return remote(psend.at[1, t], precv.at[1, t], psem_s.at[1, t], psem_r.at[1, t], (me_g - 1, me_t))

    for at in range(planes * frames):
        z, t = divmod(at, frames)
        if t == 0:
            g_right[z].wait_recv()
        if t == frames - 1:
            g_left[z].wait_recv()
        around = g3[t, z]
        hgrad = (tn(tw, around) * slope[t, z]).astype(BF16)
        ssum = nt(hgrad, cols[t, z * window : (z + 3) * window, :])
        tsum = nt(act[t, z], around)
        bsum = jnp.sum(hgrad.astype(F32), axis=1, keepdims=True)

        def add(tile, lo, width, value):
            if at > 0:
                value = acc[tile, :, lo : lo + width] + value
            acc[tile, :, lo : lo + width] = value

        for tile in range(temporal):
            width = min(LANES, 3 * window - tile * LANES)
            add(tile, 0, width, ssum[:, tile * LANES : tile * LANES + width])
            if width < LANES and at == 0:
                acc[tile, :, width:LANES] = jnp.zeros((hid, LANES - width), F32)
        add(temporal, 0, 3 * half, tsum)
        add(temporal, 3 * half, LANES - 3 * half, jnp.broadcast_to(bsum, (hid, LANES - 3 * half)))
        if at == planes * frames - 1:
            for tile in range(temporal + 1, tiles):
                acc[tile] = jnp.zeros((hid, LANES), F32)
            accb[...] = acc[...].astype(BF16)
            for _, copy in scatter:
                copy.start()
        unfold(hgrad, hcols.at[at], 0)
        parts[t, z] = nn(back, hcols[at])
        if z == 0:
            psend[1, t] = parts[t, z, 0:half, :].astype(BF16)
            pl.when(has_l)(p_left(t).start)
        if z == planes - 1:
            psend[0, t] = parts[t, z, 2 * half : 3 * half, :].astype(BF16)
            pl.when(has_r)(p_right(t).start)

    total = acc[span(near_me)]
    for j, copy in scatter:
        copy.wait_recv()
        total = total + first[j - 1].astype(F32)
    second[pl.ds(far_me, 1)] = total.astype(BF16)[None]
    for copy in share:
        copy.start()

    for load in loads[3:]:
        load.wait()

    @pl.when(has_l)
    def _():
        for t in range(frames):
            p_right(t).wait_recv()

    @pl.when(jnp.logical_not(has_l))
    def _():
        precv[0] = jnp.zeros_like(precv[0])

    @pl.when(has_r)
    def _():
        for t in range(frames):
            p_left(t).wait_recv()

    @pl.when(jnp.logical_not(has_r))
    def _():
        precv[1] = jnp.zeros_like(precv[1])

    for t in range(frames):
        for z in range(planes):
            total = parts[t, z, half : 2 * half, :]
            total = total + (parts[t, z - 1, 2 * half : 3 * half, :] if z > 0 else precv[0, t].astype(F32))
            total = total + (parts[t, z + 1, 0:half, :] if z < planes - 1 else precv[1, t].astype(F32))
            gin_ref[t, z] = (g1_ref[t, z].astype(F32) + total).astype(BF16)

    for copy in share:
        copy.wait_recv()
    total = second[0].astype(F32)
    for j in range(1, far_count):
        total = total + second[j].astype(F32)
    fin[span(near_me)] = total.astype(BF16)
    for copy in gather:
        copy.start()

    for z in range(planes):
        m_left[z].wait_recv()
        m_right[z].wait_recv()
        for t in range(frames):
            total = mown[t, z, half : 2 * half, :]
            total = total + (mown[t - 1, z, 0:half, :] if t > 0 else mrecv[0, z].astype(F32))
            total = total + (mown[t + 1, z, 2 * half : 3 * half, :] if t < frames - 1 else mrecv[1, z].astype(F32))
            rebuilt_ref[t, z] = (y2_ref[t, z].astype(F32) - total).astype(BF16)

    for t in range(frames):
        pl.when(has_r)(y_right[t].wait_send)
        pl.when(has_l)(y_left[t].wait_send)
        pl.when(has_r)(p_right(t).wait_send)
        pl.when(has_l)(p_left(t).wait_send)
    for copy in g_left + g_right + m_left + m_right + [copy for _, copy in scatter] + share:
        copy.wait_send()
    for copy in gather:
        copy.wait_recv()
    for copy in gather:
        copy.wait_send()


def finish(factor, rebuilt_in, gin_in, fin, rebuilt_ref, gin_ref, gs_ref, gb_ref, gt_ref, sem):
    copies = [
        pltpu.make_async_copy(rebuilt_in, rebuilt_ref, sem.at[0]),
        pltpu.make_async_copy(gin_in, gin_ref, sem.at[1]),
    ]
    for copy in copies:
        copy.start()
    hid, window = gs_ref.shape[1], gs_ref.shape[2]
    half = window // 9
    temporal = sum_layout(half, 1)[0]
    wide = jnp.concatenate([fin[tile].astype(F32) * factor for tile in range(temporal)], axis=1)
    for dz in range(3):
        gs_ref[dz] = wide[:, dz * window : (dz + 1) * window]
    turned = (fin[temporal].astype(F32) * factor).T
    for k in range(3):
        gt_ref[k] = turned[k * half : (k + 1) * half]
    gb_ref[...] = turned[3 * half : 3 * half + 1]
    for copy in copies:
        copy.wait()


def shards(gz_count, ta_count, outputs_fwd, cotangent, spatial_weight, hidden_bias, temporal_weight):
    frames, planes, channels, pix = outputs_fwd.shape
    half = channels // 2
    hid = spatial_weight.shape[1]
    window = 9 * half
    tw = temporal_weight.reshape((3 * half, hid))
    factor = 1.0 / math.sqrt(frames * ta_count * planes * gz_count * ROWS * COLS)
    vmem = pl.BlockSpec(memory_space=pltpu.VMEM)
    hbm = pl.BlockSpec(memory_space=pltpu.HBM)
    near_bits, far_bits = groups_of(gz_count, ta_count)
    near_count, far_count = 1 << len(near_bits), 1 << len(far_bits)
    tiles = sum_layout(half, near_count)[1]
    per = tiles // near_count
    dma = pltpu.SemaphoreType.DMA
    field = jax.ShapeDtypeStruct((frames, planes, half, pix), BF16)
    held = pltpu.VMEM((frames, planes, half, pix), BF16)
    outs = pl.pallas_call(
        functools.partial(kernel, gz_count, ta_count),
        out_shape=(held, held, pltpu.VMEM((tiles, hid, LANES), BF16)),
        in_specs=[hbm] * 5,
        out_specs=(vmem,) * 3,
        scratch_shapes=[
            pltpu.VMEM((frames, (planes + 2) * window, pix), BF16),
            pltpu.VMEM((frames * planes, 9 * hid, pix), BF16),
            pltpu.VMEM((frames, planes, 3 * half, pix), BF16),
            pltpu.VMEM((2, frames, half, pix), BF16),
            pltpu.VMEM((frames, planes, hid, pix), F32),
            pltpu.VMEM((frames, planes, hid, pix), BF16),
            pltpu.VMEM((frames, planes, 3 * half, pix), F32),
            pltpu.VMEM((frames, planes, 3 * half, pix), F32),
            pltpu.VMEM((2, planes, half, pix), BF16),
            pltpu.VMEM((2, planes, half, pix), BF16),
            pltpu.VMEM((2, frames, half, pix), BF16),
            pltpu.VMEM((2, frames, half, pix), BF16),
            pltpu.VMEM((frames, planes, half, pix), BF16),
            pltpu.VMEM((frames, planes, half, pix), BF16),
            pltpu.VMEM((frames, planes, half, pix), BF16),
            pltpu.VMEM(spatial_weight.shape, BF16),
            pltpu.VMEM((1, hid), F32),
            pltpu.VMEM(tw.shape, BF16),
            pltpu.VMEM((hid, 3 * window), BF16),
            pltpu.VMEM((3 * half, 9 * hid), BF16),
            pltpu.VMEM((tiles, hid, LANES), F32),
            pltpu.VMEM((tiles, hid, LANES), BF16),
            pltpu.VMEM((near_count - 1, per, hid, LANES), BF16),
            pltpu.VMEM((far_count, per, hid, LANES), BF16),
            dma((5,)), dma((frames,)), dma((frames, 3)),
            dma((2, frames)), dma((2, frames)), dma((2, planes)), dma((2, planes)),
            dma((2, planes)), dma((2, planes)), dma((2, frames)), dma((2, frames)),
            dma((near_count - 1,)), dma((near_count - 1,)),
            dma((far_count - 1,)), dma((far_count - 1,)),
            dma((near_count - 1,)), dma((near_count - 1,)),
        ],
        compiler_params=pltpu.CompilerParams(
            collective_id=0, has_side_effects=True, vmem_limit_bytes=60 * 1024 * 1024
        ),
    )(outputs_fwd, cotangent, spatial_weight, hidden_bias[None, :], tw)
    ends = pl.pallas_call(
        functools.partial(finish, factor),
        out_shape=(
            field,
            field,
            jax.ShapeDtypeStruct((3, hid, window), F32),
            jax.ShapeDtypeStruct((1, hid), F32),
            jax.ShapeDtypeStruct((3, half, hid), F32),
        ),
        in_specs=[vmem] * 3,
        out_specs=(hbm,) * 2 + (vmem,) * 3,
        scratch_shapes=[dma((2,))],
        compiler_params=pltpu.CompilerParams(vmem_limit_bytes=16 * 1024 * 1024),
    )(*outs)
    return ends[0], ends[1], ends[2], ends[3].reshape((hid,)), ends[4]


def solution(mesh):
    placed = (P("ta", "gz", None, None), P("ta", "gz", None, None), P(), P(), P())
    return jax.shard_map(
        functools.partial(shards, mesh.shape["gz"], mesh.shape["ta"]),
        mesh=mesh,
        in_specs=placed,
        out_specs=(P("ta", "gz", None, None), P("ta", "gz", None, None), P(), P(), P()),
        check_vma=False,
    )
```

```python
import functools
import math

import jax
import jax.numpy as jnp
from jax import lax
from jax.experimental import pallas as pl
from jax.experimental.pallas import tpu as pltpu
from jax.sharding import PartitionSpec as P

ROWS = 8
COLS = 160
LANES = 128
F32 = jnp.float32
BF16 = jnp.bfloat16


def groups_of(gz_count, ta_count):
    bits = lambda count: [1 << i for i in range(count.bit_length() - 1)]
    gz_bits = [("gz", bit) for bit in bits(gz_count)]
    ta_bits = [("ta", bit) for bit in bits(ta_count)]
    return gz_bits[:3], gz_bits[3:] + ta_bits


def sum_layout(half, near_count):
    temporal = -(-27 * half // LANES)
    tiles = temporal + -(-(3 * half + 1) // LANES)
    return temporal, -(-tiles // near_count) * near_count


def nn(lhs, rhs):
    return lax.dot_general(lhs, rhs, (((1,), (0,)), ((), ())), preferred_element_type=F32)


def nt(lhs, rhs):
    return lax.dot_general(lhs, rhs, (((1,), (1,)), ((), ())), preferred_element_type=F32)


def tn(lhs, rhs):
    return lax.dot_general(lhs, rhs, (((0,), (0,)), ((), ())), preferred_element_type=F32)


def kernel(
    gz_count, ta_count,
    x_hbm, g_hbm, sw_hbm, bias_hbm, tw_hbm,
    rebuilt_ref, gin_ref, fin,
    cols, hcols, g3, yh, slope, act, hgr, parts, mown, msend, mrecv, psend, precv,
    y_ref, y2_ref, g1_ref, sw_ref, bias_ref, tw_ref, wcat, flip, acc, accb, first, second,
    lsem, ysem, g3sem,
    ysem_s, ysem_r, gsem_s, gsem_r, msem_s, msem_r, psem_s, psem_r,
    asem_s, asem_r, bsem_s, bsem_r, csem_s, csem_r,
):
    frames, planes, half, pix = y_ref.shape
    hid = bias_ref.shape[1]
    window = 9 * half
    me_g = lax.axis_index("gz")
    me_t = lax.axis_index("ta")
    has_l = me_g > 0
    has_r = me_g < gz_count - 1
    mesh_id = pl.DeviceIdType.MESH
    ta_r = lax.rem(me_t + 1, ta_count)
    ta_l = lax.rem(me_t + ta_count - 1, ta_count)
    near_bits, far_bits = groups_of(gz_count, ta_count)

    def member(group, flip_mask):
        place = {"gz": me_g, "ta": me_t}
        index = 0
        for order, (axis, bit) in enumerate(group):
            at = me_g if axis == "gz" else me_t
            has = lax.rem(at // bit, 2)
            if flip_mask >> order & 1:
                place[axis] = place[axis] + bit - 2 * bit * has
                has = 1 - has
            index = index + (has << order)
        return (place["gz"], place["ta"]), index

    near_count, far_count = 1 << len(near_bits), 1 << len(far_bits)
    barrier = pltpu.get_barrier_semaphore()

    def greet(dev):
        pl.semaphore_signal(barrier, inc=1, device_id=dev, device_id_type=mesh_id)

    greet((me_g, ta_r))
    greet((me_g, ta_l))

    @pl.when(has_l)
    def _():
        greet((me_g - 1, me_t))

    @pl.when(has_r)
    def _():
        greet((me_g + 1, me_t))

    for j in range(1, near_count):
        greet(member(near_bits, j)[0])
    for j in range(1, far_count):
        greet(member(far_bits, j)[0])

    pairs = (
        (sw_hbm, sw_ref), (tw_hbm, tw_ref), (bias_hbm, bias_ref),
        (x_hbm.at[:, :, half : 2 * half], y2_ref), (g_hbm.at[:, :, 0:half], g1_ref),
    )
    loads = [pltpu.make_async_copy(src, dst, lsem.at[i]) for i, (src, dst) in enumerate(pairs)]
    own = [pltpu.make_async_copy(x_hbm.at[t, :, 0:half], y_ref.at[t], ysem.at[t]) for t in range(frames)]
    local = [
        (s, k, pltpu.make_async_copy(
            g_hbm.at[s + 1 - k, :, half : 2 * half], g3.at[s, :, k * half : (k + 1) * half], g3sem.at[s, k]
        ))
        for s in range(frames) for k in range(3) if 0 <= s + 1 - k < frames
    ]
    for load in own + loads[:3]:
        load.start()
    beside = has_l.astype(jnp.int32) + has_r.astype(jnp.int32)
    pl.semaphore_wait(barrier, near_count + far_count + beside)

    def remote(src, dst, ssem, rsem, dev):
        return pltpu.make_async_remote_copy(
            src_ref=src, dst_ref=dst, send_sem=ssem, recv_sem=rsem, device_id=dev, device_id_type=mesh_id
        )

    y_right = [
        remote(x_hbm.at[t, planes - 1, 0:half], yh.at[0, t], ysem_s.at[0, t], ysem_r.at[0, t], (me_g + 1, me_t))
        for t in range(frames)
    ]
    y_left = [
        remote(x_hbm.at[t, 0, 0:half], yh.at[1, t], ysem_s.at[1, t], ysem_r.at[1, t], (me_g - 1, me_t))
        for t in range(frames)
    ]
    g_left = [
        remote(
            g_hbm.at[0, z, half : 2 * half], g3.at[frames - 1, z, 0:half],
            gsem_s.at[0, z], gsem_r.at[0, z], (me_g, ta_l),
        )
        for z in range(planes)
    ]
    g_right = [
        remote(
            g_hbm.at[frames - 1, z, half : 2 * half], g3.at[0, z, 2 * half : 3 * half],
            gsem_s.at[1, z], gsem_r.at[1, z], (me_g, ta_r),
        )
        for z in range(planes)
    ]
    g_right[0].start()
    for t in range(frames):
        pl.when(has_r)(y_right[t].start)
        pl.when(has_l)(y_left[t].start)
    g_left[0].start()
    for z in range(1, planes):
        g_right[z].start()
        g_left[z].start()
    for _, _, load in local:
        load.start()
    for load in loads[3:]:
        load.start()

    for load in loads[:3]:
        load.wait()
    for dz in range(3):
        wcat[:, dz * window : (dz + 1) * window] = sw_ref[dz]
        turned = sw_ref[dz].astype(F32).T.astype(BF16)
        for w in range(9):
            flip[dz * half : (dz + 1) * half, w * hid : (w + 1) * hid] = turned[(8 - w) * half : (9 - w) * half]
    bias = jnp.broadcast_to(bias_ref[...], (8, hid)).T[:, 0:1]

    place = lax.broadcasted_iota(jnp.int32, (1, pix), 1)
    column = lax.rem(place, COLS)
    col_ok = {-1: column < COLS - 1, 1: column > 0}
    edge = -(-COLS // LANES) * LANES
    zero = jnp.zeros((), BF16)
    head_ok = place[:, 0:edge] >= COLS
    tail_ok = place[:, pix - edge : pix] < pix - COLS

    def unfold(value, out, base):
        rows = value.shape[0]
        for c in (-1, 0, 1):
            source = value if c == 0 else jnp.where(col_ok[c], value, zero)
            for r in (-1, 0, 1):
                shift = (-(r * COLS + c)) % pix
                moved = pltpu.roll(source, shift, 1) if shift else source
                at = pl.ds(base + (3 * (r + 1) + c + 1) * rows, rows)
                if r == -1:
                    out[at, 0:edge] = jnp.where(head_ok, moved[:, 0:edge], zero)
                    out[at, edge:pix] = moved[:, edge:pix]
                elif r == 1:
                    out[at, 0 : pix - edge] = moved[:, 0 : pix - edge]
                    out[at, pix - edge : pix] = jnp.where(tail_ok, moved[:, pix - edge : pix], zero)
                else:
                    out[at, :] = moved

    for t in range(frames):
        own[t].wait()
        for z in range(planes):
            unfold(y_ref[t, z], cols.at[t], (z + 1) * window)

    whole = wcat[...]
    tw = tw_ref[...]
    for t in range(frames):
        for z in range(planes):
            lo, hi = max(z, 1), min(z + 3, planes + 1)
            slope[t, z] = nn(whole[:, (lo - z) * window : (hi - z) * window], cols[t, lo * window : hi * window, :]) + bias

    temporal = sum_layout(half, near_count)[0]
    tiles = acc.shape[0]
    per = tiles // near_count

    def span(index):
        return pl.ds(index * per, per)

    near_me = member(near_bits, 0)[1]
    far_me = member(far_bits, 0)[1]
    scatter, share, gather = [], [], []
    for j in reversed(range(1, near_count)):
        dev, index = member(near_bits, j)
        scatter.append((j, remote(accb.at[span(index)], first.at[j - 1], asem_s.at[j - 1], asem_r.at[j - 1], dev)))
        mine = fin.at[span(near_me)]
        gather.append(remote(mine, mine, csem_s.at[j - 1], csem_r.at[j - 1], dev))
    for j in reversed(range(1, far_count)):
        dev, _ = member(far_bits, j)
        share.append(remote(second.at[far_me], second.at[far_me], bsem_s.at[j - 1], bsem_r.at[j - 1], dev))

    back = flip[...]

    def p_right(t):
        return remote(psend.at[0, t], precv.at[0, t], psem_s.at[0, t], psem_r.at[0, t], (me_g + 1, me_t))

    def p_left(t):
        return remote(psend.at[1, t], precv.at[1, t], psem_s.at[1, t], psem_r.at[1, t], (me_g - 1, me_t))

    m_right = [
        remote(msend.at[0, z], mrecv.at[0, z], msem_s.at[0, z], msem_r.at[0, z], (me_g, ta_r)) for z in range(planes)
    ]
    m_left = [
        remote(msend.at[1, z], mrecv.at[1, z], msem_s.at[1, z], msem_r.at[1, z], (me_g, ta_l)) for z in range(planes)
    ]

    def halo(t, side, has, copy):
        base = side * (planes + 1) * window

        @pl.when(has)
        def _():
            copy.wait_recv()
            unfold(yh[side, t], cols.at[t], base)

        @pl.when(jnp.logical_not(has))
        def _():
            cols[t, base : base + window, :] = jnp.zeros((window, pix), BF16)

    def forward(t, z):
        pre = slope[t, z]
        if z == 0:
            pre = pre + nn(whole[:, 0:window], cols[t, 0:window, :])
        if z == planes - 1:
            pre = pre + nn(whole[:, 2 * window : 3 * window], cols[t, (planes + 1) * window : (planes + 2) * window, :])
        sig = jax.nn.sigmoid(pre)
        active = (pre * sig).astype(BF16)
        slope[t, z] = sig * (1.0 + pre * (1.0 - sig))
        act[t, z] = active
        mapped = nn(tw, active)
        mown[t, z] = mapped
        if t == 0:
            msend[1, z] = mapped[2 * half : 3 * half, :].astype(BF16)
            m_left[z].start()
        if t == frames - 1:
            msend[0, z] = mapped[0:half, :].astype(BF16)
            m_right[z].start()

    def sums(t, z, fresh):
        if t == 0:
            g_right[z].wait_recv()
        if t == frames - 1:
            g_left[z].wait_recv()
        around = g3[t, z]
        hgrad = (tn(tw, around) * slope[t, z]).astype(BF16)
        hgr[t, z] = hgrad
        ssum = nt(hgrad, cols[t, z * window : (z + 3) * window, :])
        tsum = nt(act[t, z], around)
        bsum = jnp.sum(hgrad.astype(F32), axis=1, keepdims=True)

        def add(tile, lo, width, value):
            if not fresh:
                value = acc[tile, :, lo : lo + width] + value
            acc[tile, :, lo : lo + width] = value

        for tile in range(temporal):
            width = min(LANES, 3 * window - tile * LANES)
            add(tile, 0, width, ssum[:, tile * LANES : tile * LANES + width])
            if width < LANES and fresh:
                acc[tile, :, width:LANES] = jnp.zeros((hid, LANES - width), F32)
        add(temporal, 0, 3 * half, tsum)
        add(temporal, 3 * half, LANES - 3 * half, jnp.broadcast_to(bsum, (hid, LANES - 3 * half)))

    def adjoint(t, z):
        at = t * planes + z
        unfold(hgr[t, z], hcols.at[at], 0)
        parts[t, z] = nn(back, hcols[at])
        if z == 0:
            psend[1, t] = parts[t, z, 0:half, :].astype(BF16)
        if z == planes - 1:
            psend[0, t] = parts[t, z, 2 * half : 3 * half, :].astype(BF16)

    for t in range(frames):
        halo(t, 0, has_l, y_right[t])
        halo(t, 1, has_r, y_left[t])
        for z in range(planes):
            forward(t, z)
        if t == 0:
            for _, _, load in local:
                load.wait()
        sums(t, 0, t == 0)
    rest = [(t, z) for z in range(1, planes) for t in range(frames)]
    for t, z in rest[:-1]:
        sums(t, z, False)
    done = [(t, 0) for t in range(frames)] + rest
    if rest:
        sums(*rest[-1], False)
    for tile in range(temporal + 1, tiles):
        acc[tile] = jnp.zeros((hid, LANES), F32)
    accb[...] = acc[...].astype(BF16)
    for _, copy in scatter:
        copy.start()
    for t, z in done:
        adjoint(t, z)

    total = acc[span(near_me)]
    for j, copy in scatter:
        copy.wait_recv()
        total = total + first[j - 1].astype(F32)
    second[pl.ds(far_me, 1)] = total.astype(BF16)[None]
    for copy in share:
        copy.start()
    for t in range(frames):
        pl.when(has_l)(p_left(t).start)
        pl.when(has_r)(p_right(t).start)

    for load in loads[3:]:
        load.wait()

    for copy in share:
        copy.wait_recv()
    total = second[0].astype(F32)
    for j in range(1, far_count):
        total = total + second[j].astype(F32)
    fin[span(near_me)] = total.astype(BF16)
    for copy in gather:
        copy.start()

    for z in range(planes):
        m_left[z].wait_recv()
        m_right[z].wait_recv()
        for t in range(frames):
            total = mown[t, z, half : 2 * half, :]
            total = total + (mown[t - 1, z, 0:half, :] if t > 0 else mrecv[0, z].astype(F32))
            total = total + (mown[t + 1, z, 2 * half : 3 * half, :] if t < frames - 1 else mrecv[1, z].astype(F32))
            rebuilt_ref[t, z] = (y2_ref[t, z].astype(F32) - total).astype(BF16)

    @pl.when(has_l)
    def _():
        for t in range(frames):
            p_right(t).wait_recv()

    @pl.when(jnp.logical_not(has_l))
    def _():
        precv[0] = jnp.zeros_like(precv[0])

    @pl.when(has_r)
    def _():
        for t in range(frames):
            p_left(t).wait_recv()

    @pl.when(jnp.logical_not(has_r))
    def _():
        precv[1] = jnp.zeros_like(precv[1])

    for t in range(frames):
        for z in range(planes):
            total = parts[t, z, half : 2 * half, :]
            total = total + (parts[t, z - 1, 2 * half : 3 * half, :] if z > 0 else precv[0, t].astype(F32))
            total = total + (parts[t, z + 1, 0:half, :] if z < planes - 1 else precv[1, t].astype(F32))
            gin_ref[t, z] = (g1_ref[t, z].astype(F32) + total).astype(BF16)

    for t in range(frames):
        pl.when(has_r)(y_right[t].wait_send)
        pl.when(has_l)(y_left[t].wait_send)
        pl.when(has_r)(p_right(t).wait_send)
        pl.when(has_l)(p_left(t).wait_send)
    for copy in g_left + g_right + m_left + m_right + [copy for _, copy in scatter] + share:
        copy.wait_send()
    for copy in gather:
        copy.wait_recv()
    for copy in gather:
        copy.wait_send()


def finish(factor, rebuilt_in, gin_in, fin, rebuilt_ref, gin_ref, gs_ref, gb_ref, gt_ref, sem):
    copies = [
        pltpu.make_async_copy(rebuilt_in, rebuilt_ref, sem.at[0]),
        pltpu.make_async_copy(gin_in, gin_ref, sem.at[1]),
    ]
    for copy in copies:
        copy.start()
    hid, window = gs_ref.shape[1], gs_ref.shape[2]
    half = window // 9
    temporal = sum_layout(half, 1)[0]
    wide = jnp.concatenate([fin[tile].astype(F32) * factor for tile in range(temporal)], axis=1)
    for dz in range(3):
        gs_ref[dz] = wide[:, dz * window : (dz + 1) * window]
    turned = (fin[temporal].astype(F32) * factor).T
    for k in range(3):
        gt_ref[k] = turned[k * half : (k + 1) * half]
    gb_ref[...] = turned[3 * half : 3 * half + 1]
    for copy in copies:
        copy.wait()


def shards(gz_count, ta_count, outputs_fwd, cotangent, spatial_weight, hidden_bias, temporal_weight):
    frames, planes, channels, pix = outputs_fwd.shape
    half = channels // 2
    hid = spatial_weight.shape[1]
    window = 9 * half
    tw = temporal_weight.reshape((3 * half, hid))
    factor = 1.0 / math.sqrt(frames * ta_count * planes * gz_count * ROWS * COLS)
    vmem = pl.BlockSpec(memory_space=pltpu.VMEM)
    hbm = pl.BlockSpec(memory_space=pltpu.HBM)
    near_bits, far_bits = groups_of(gz_count, ta_count)
    near_count, far_count = 1 << len(near_bits), 1 << len(far_bits)
    tiles = sum_layout(half, near_count)[1]
    per = tiles // near_count
    dma = pltpu.SemaphoreType.DMA
    field = jax.ShapeDtypeStruct((frames, planes, half, pix), BF16)
    held = pltpu.VMEM((frames, planes, half, pix), BF16)
    outs = pl.pallas_call(
        functools.partial(kernel, gz_count, ta_count),
        out_shape=(held, held, pltpu.VMEM((tiles, hid, LANES), BF16)),
        in_specs=[hbm] * 5,
        out_specs=(vmem,) * 3,
        scratch_shapes=[
            pltpu.VMEM((frames, (planes + 2) * window, pix), BF16),
            pltpu.VMEM((frames * planes, 9 * hid, pix), BF16),
            pltpu.VMEM((frames, planes, 3 * half, pix), BF16),
            pltpu.VMEM((2, frames, half, pix), BF16),
            pltpu.VMEM((frames, planes, hid, pix), F32),
            pltpu.VMEM((frames, planes, hid, pix), BF16),
            pltpu.VMEM((frames, planes, hid, pix), BF16),
            pltpu.VMEM((frames, planes, 3 * half, pix), F32),
            pltpu.VMEM((frames, planes, 3 * half, pix), F32),
            pltpu.VMEM((2, planes, half, pix), BF16),
            pltpu.VMEM((2, planes, half, pix), BF16),
            pltpu.VMEM((2, frames, half, pix), BF16),
            pltpu.VMEM((2, frames, half, pix), BF16),
            pltpu.VMEM((frames, planes, half, pix), BF16),
            pltpu.VMEM((frames, planes, half, pix), BF16),
            pltpu.VMEM((frames, planes, half, pix), BF16),
            pltpu.VMEM(spatial_weight.shape, BF16),
            pltpu.VMEM((1, hid), F32),
            pltpu.VMEM(tw.shape, BF16),
            pltpu.VMEM((hid, 3 * window), BF16),
            pltpu.VMEM((3 * half, 9 * hid), BF16),
            pltpu.VMEM((tiles, hid, LANES), F32),
            pltpu.VMEM((tiles, hid, LANES), BF16),
            pltpu.VMEM((near_count - 1, per, hid, LANES), BF16),
            pltpu.VMEM((far_count, per, hid, LANES), BF16),
            dma((5,)), dma((frames,)), dma((frames, 3)),
            dma((2, frames)), dma((2, frames)), dma((2, planes)), dma((2, planes)),
            dma((2, planes)), dma((2, planes)), dma((2, frames)), dma((2, frames)),
            dma((near_count - 1,)), dma((near_count - 1,)),
            dma((far_count - 1,)), dma((far_count - 1,)),
            dma((near_count - 1,)), dma((near_count - 1,)),
        ],
        compiler_params=pltpu.CompilerParams(
            collective_id=0, has_side_effects=True, vmem_limit_bytes=60 * 1024 * 1024
        ),
    )(outputs_fwd, cotangent, spatial_weight, hidden_bias[None, :], tw)
    ends = pl.pallas_call(
        functools.partial(finish, factor),
        out_shape=(
            field,
            field,
            jax.ShapeDtypeStruct((3, hid, window), F32),
            jax.ShapeDtypeStruct((1, hid), F32),
            jax.ShapeDtypeStruct((3, half, hid), F32),
        ),
        in_specs=[vmem] * 3,
        out_specs=(hbm,) * 2 + (vmem,) * 3,
        scratch_shapes=[dma((2,))],
        compiler_params=pltpu.CompilerParams(vmem_limit_bytes=16 * 1024 * 1024),
    )(*outs)
    return ends[0], ends[1], ends[2], ends[3].reshape((hid,)), ends[4]


def solution(mesh):
    placed = (P("ta", "gz", None, None), P("ta", "gz", None, None), P(), P(), P())
    return jax.shard_map(
        functools.partial(shards, mesh.shape["gz"], mesh.shape["ta"]),
        mesh=mesh,
        in_specs=placed,
        out_specs=(P("ta", "gz", None, None), P("ta", "gz", None, None), P(), P(), P()),
        check_vma=False,
    )
```

```python
import functools
import math

import jax
import jax.numpy as jnp
from jax import lax
from jax.experimental import pallas as pl
from jax.experimental.pallas import tpu as pltpu
from jax.sharding import PartitionSpec as P

ROWS = 8
COLS = 160
LANES = 128
F32 = jnp.float32
BF16 = jnp.bfloat16


def groups_of(gz_count, ta_count):
    bits = lambda count: [1 << i for i in range(count.bit_length() - 1)]
    gz_bits = [("gz", bit) for bit in bits(gz_count)]
    ta_bits = [("ta", bit) for bit in bits(ta_count)]
    return gz_bits[:3], gz_bits[3:] + ta_bits


def sum_layout(half, near_count):
    temporal = -(-27 * half // LANES)
    tiles = temporal + -(-(3 * half + 1) // LANES)
    return temporal, -(-tiles // near_count) * near_count


def nn(lhs, rhs):
    return lax.dot_general(lhs, rhs, (((1,), (0,)), ((), ())), preferred_element_type=F32)


def nt(lhs, rhs):
    return lax.dot_general(lhs, rhs, (((1,), (1,)), ((), ())), preferred_element_type=F32)


def tn(lhs, rhs):
    return lax.dot_general(lhs, rhs, (((0,), (0,)), ((), ())), preferred_element_type=F32)


def kernel(
    gz_count, ta_count,
    x_hbm, g_hbm, sw_hbm, bias_hbm, tw_hbm,
    rebuilt_ref, gin_ref, fin,
    cols, hcols, g3, yh, slope, act, hgr, parts, mown, msend, mrecv, psend, precv,
    y_ref, y2_ref, g1_ref, sw_ref, bias_ref, tw_ref, wcat, flip, acc, accb, first, second,
    lsem, ysem, g3sem,
    ysem_s, ysem_r, gsem_s, gsem_r, msem_s, msem_r, psem_s, psem_r,
    asem_s, asem_r, bsem_s, bsem_r, csem_s, csem_r,
):
    frames, planes, half, pix = y_ref.shape
    hid = bias_ref.shape[1]
    window = 9 * half
    me_g = lax.axis_index("gz")
    me_t = lax.axis_index("ta")
    has_l = me_g > 0
    has_r = me_g < gz_count - 1
    mesh_id = pl.DeviceIdType.MESH
    ta_r = lax.rem(me_t + 1, ta_count)
    ta_l = lax.rem(me_t + ta_count - 1, ta_count)
    near_bits, far_bits = groups_of(gz_count, ta_count)

    def member(group, flip_mask):
        place = {"gz": me_g, "ta": me_t}
        index = 0
        for order, (axis, bit) in enumerate(group):
            at = me_g if axis == "gz" else me_t
            has = lax.rem(at // bit, 2)
            if flip_mask >> order & 1:
                place[axis] = place[axis] + bit - 2 * bit * has
                has = 1 - has
            index = index + (has << order)
        return (place["gz"], place["ta"]), index

    near_count, far_count = 1 << len(near_bits), 1 << len(far_bits)
    barrier = pltpu.get_barrier_semaphore()

    def greet(dev):
        pl.semaphore_signal(barrier, inc=1, device_id=dev, device_id_type=mesh_id)

    greet((me_g, ta_r))
    greet((me_g, ta_l))

    @pl.when(has_l)
    def _():
        greet((me_g - 1, me_t))

    @pl.when(has_r)
    def _():
        greet((me_g + 1, me_t))

    for j in range(1, near_count):
        greet(member(near_bits, j)[0])
    for j in range(1, far_count):
        greet(member(far_bits, j)[0])

    pairs = (
        (sw_hbm, sw_ref), (tw_hbm, tw_ref), (bias_hbm, bias_ref),
        (x_hbm.at[:, :, half : 2 * half], y2_ref), (g_hbm.at[:, :, 0:half], g1_ref),
    )
    loads = [pltpu.make_async_copy(src, dst, lsem.at[i]) for i, (src, dst) in enumerate(pairs)]
    own = [pltpu.make_async_copy(x_hbm.at[t, :, 0:half], y_ref.at[t], ysem.at[t]) for t in range(frames)]
    local = [
        (s, k, pltpu.make_async_copy(
            g_hbm.at[s + 1 - k, :, half : 2 * half], g3.at[s, :, k * half : (k + 1) * half], g3sem.at[s, k]
        ))
        for s in range(frames) for k in range(3) if 0 <= s + 1 - k < frames
    ]
    for load in own + loads[:3]:
        load.start()
    beside = has_l.astype(jnp.int32) + has_r.astype(jnp.int32)
    pl.semaphore_wait(barrier, near_count + far_count + beside)

    def remote(src, dst, ssem, rsem, dev):
        return pltpu.make_async_remote_copy(
            src_ref=src, dst_ref=dst, send_sem=ssem, recv_sem=rsem, device_id=dev, device_id_type=mesh_id
        )

    y_right = [
        remote(x_hbm.at[t, planes - 1, 0:half], yh.at[0, t], ysem_s.at[0, t], ysem_r.at[0, t], (me_g + 1, me_t))
        for t in range(frames)
    ]
    y_left = [
        remote(x_hbm.at[t, 0, 0:half], yh.at[1, t], ysem_s.at[1, t], ysem_r.at[1, t], (me_g - 1, me_t))
        for t in range(frames)
    ]
    g_left = [
        remote(
            g_hbm.at[0, z, half : 2 * half], g3.at[frames - 1, z, 0:half],
            gsem_s.at[0, z], gsem_r.at[0, z], (me_g, ta_l),
        )
        for z in range(planes)
    ]
    g_right = [
        remote(
            g_hbm.at[frames - 1, z, half : 2 * half], g3.at[0, z, 2 * half : 3 * half],
            gsem_s.at[1, z], gsem_r.at[1, z], (me_g, ta_r),
        )
        for z in range(planes)
    ]
    g_right[0].start()
    for t in range(frames):
        pl.when(has_r)(y_right[t].start)
        pl.when(has_l)(y_left[t].start)
    g_left[0].start()
    for z in range(1, planes):
        g_right[z].start()
        g_left[z].start()
    for _, _, load in local:
        load.start()
    for load in loads[3:]:
        load.start()

    for load in loads[:3]:
        load.wait()
    for dz in range(3):
        wcat[:, dz * window : (dz + 1) * window] = sw_ref[dz]
        turned = sw_ref[dz].astype(F32).T.astype(BF16)
        for w in range(9):
            flip[dz * half : (dz + 1) * half, w * hid : (w + 1) * hid] = turned[(8 - w) * half : (9 - w) * half]
    bias = jnp.broadcast_to(bias_ref[...], (8, hid)).T[:, 0:1]

    place = lax.broadcasted_iota(jnp.int32, (1, pix), 1)
    column = lax.rem(place, COLS)
    col_ok = {-1: column < COLS - 1, 1: column > 0}
    edge = -(-COLS // LANES) * LANES
    zero = jnp.zeros((), BF16)
    head_ok = place[:, 0:edge] >= COLS
    tail_ok = place[:, pix - edge : pix] < pix - COLS

    def unfold(value, out, base):
        rows = value.shape[0]
        for c in (-1, 0, 1):
            source = value if c == 0 else jnp.where(col_ok[c], value, zero)
            for r in (-1, 0, 1):
                shift = (-(r * COLS + c)) % pix
                moved = pltpu.roll(source, shift, 1) if shift else source
                at = pl.ds(base + (3 * (r + 1) + c + 1) * rows, rows)
                if r == -1:
                    out[at, 0:edge] = jnp.where(head_ok, moved[:, 0:edge], zero)
                    out[at, edge:pix] = moved[:, edge:pix]
                elif r == 1:
                    out[at, 0 : pix - edge] = moved[:, 0 : pix - edge]
                    out[at, pix - edge : pix] = jnp.where(tail_ok, moved[:, pix - edge : pix], zero)
                else:
                    out[at, :] = moved

    for t in range(frames):
        own[t].wait()
        for z in range(planes):
            unfold(y_ref[t, z], cols.at[t], (z + 1) * window)

    whole = wcat[...]
    tw = tw_ref[...]
    for t in range(frames):
        for z in range(planes):
            lo, hi = max(z, 1), min(z + 3, planes + 1)
            slope[t, z] = nn(whole[:, (lo - z) * window : (hi - z) * window], cols[t, lo * window : hi * window, :]) + bias

    temporal = sum_layout(half, near_count)[0]
    tiles = acc.shape[0]
    per = tiles // near_count

    def span(index):
        return pl.ds(index * per, per)

    near_me = member(near_bits, 0)[1]
    far_me = member(far_bits, 0)[1]
    scatter, share, gather = [], [], []
    for j in reversed(range(1, near_count)):
        dev, index = member(near_bits, j)
        scatter.append((j, remote(accb.at[span(index)], first.at[j - 1], asem_s.at[j - 1], asem_r.at[j - 1], dev)))
        mine = fin.at[span(near_me)]
        gather.append(remote(mine, mine, csem_s.at[j - 1], csem_r.at[j - 1], dev))
    for j in reversed(range(1, far_count)):
        dev, _ = member(far_bits, j)
        share.append(remote(second.at[far_me], second.at[far_me], bsem_s.at[j - 1], bsem_r.at[j - 1], dev))

    back = flip[...]

    def p_right(t):
        return remote(psend.at[0, t], precv.at[0, t], psem_s.at[0, t], psem_r.at[0, t], (me_g + 1, me_t))

    def p_left(t):
        return remote(psend.at[1, t], precv.at[1, t], psem_s.at[1, t], psem_r.at[1, t], (me_g - 1, me_t))

    m_right = [
        remote(msend.at[0, z], mrecv.at[0, z], msem_s.at[0, z], msem_r.at[0, z], (me_g, ta_r)) for z in range(planes)
    ]
    m_left = [
        remote(msend.at[1, z], mrecv.at[1, z], msem_s.at[1, z], msem_r.at[1, z], (me_g, ta_l)) for z in range(planes)
    ]

    def halo(t, side, has, copy):
        base = side * (planes + 1) * window

        @pl.when(has)
        def _():
            copy.wait_recv()
            unfold(yh[side, t], cols.at[t], base)

        @pl.when(jnp.logical_not(has))
        def _():
            cols[t, base : base + window, :] = jnp.zeros((window, pix), BF16)

    def forward(t, z):
        pre = slope[t, z]
        if z == 0:
            pre = pre + nn(whole[:, 0:window], cols[t, 0:window, :])
        if z == planes - 1:
            pre = pre + nn(whole[:, 2 * window : 3 * window], cols[t, (planes + 1) * window : (planes + 2) * window, :])
        sig = jax.nn.sigmoid(pre)
        active = (pre * sig).astype(BF16)
        slope[t, z] = sig * (1.0 + pre * (1.0 - sig))
        act[t, z] = active
        mapped = nn(tw, active)
        mown[t, z] = mapped
        if t == 0:
            msend[1, z] = mapped[2 * half : 3 * half, :].astype(BF16)
            m_left[z].start()
        if t == frames - 1:
            msend[0, z] = mapped[0:half, :].astype(BF16)
            m_right[z].start()

    def sums(t, z, fresh):
        if t == 0:
            g_right[z].wait_recv()
        if t == frames - 1:
            g_left[z].wait_recv()
        around = g3[t, z]
        hgrad = (tn(tw, around) * slope[t, z]).astype(BF16)
        hgr[t, z] = hgrad
        ssum = nt(hgrad, cols[t, z * window : (z + 3) * window, :])
        tsum = nt(act[t, z], around)
        bsum = jnp.sum(hgrad.astype(F32), axis=1, keepdims=True)

        def add(tile, lo, width, value):
            if not fresh:
                value = acc[tile, :, lo : lo + width] + value
            acc[tile, :, lo : lo + width] = value

        for tile in range(temporal):
            width = min(LANES, 3 * window - tile * LANES)
            add(tile, 0, width, ssum[:, tile * LANES : tile * LANES + width])
            if width < LANES and fresh:
                acc[tile, :, width:LANES] = jnp.zeros((hid, LANES - width), F32)
        add(temporal, 0, 3 * half, tsum)
        add(temporal, 3 * half, LANES - 3 * half, jnp.broadcast_to(bsum, (hid, LANES - 3 * half)))

    def adjoint(t, z):
        at = t * planes + z
        unfold(hgr[t, z], hcols.at[at], 0)
        parts[t, z] = nn(back, hcols[at])
        if z == 0:
            psend[1, t] = parts[t, z, 0:half, :].astype(BF16)
        if z == planes - 1:
            psend[0, t] = parts[t, z, 2 * half : 3 * half, :].astype(BF16)

    for t in range(frames):
        halo(t, 0, has_l, y_right[t])
        halo(t, 1, has_r, y_left[t])
        for z in range(planes):
            forward(t, z)
        if t == 0:
            for _, _, load in local:
                load.wait()
        sums(t, 0, t == 0)
    rest = [(t, z) for z in range(1, planes) for t in range(frames)]
    for t, z in rest[:-1]:
        sums(t, z, False)
    done = [(t, 0) for t in range(frames)] + rest
    if rest:
        sums(*rest[-1], False)
    for tile in range(temporal + 1, tiles):
        acc[tile] = jnp.zeros((hid, LANES), F32)
    accb[...] = acc[...].astype(BF16)
    for _, copy in scatter:
        copy.start()
    for t, z in done:
        adjoint(t, z)

    total = acc[span(near_me)]
    for j, copy in scatter:
        copy.wait_recv()
        total = total + first[j - 1].astype(F32)
    second[pl.ds(far_me, 1)] = total.astype(BF16)[None]
    for copy in share:
        copy.start()
    for t in range(frames):
        pl.when(has_l)(p_left(t).start)
        pl.when(has_r)(p_right(t).start)

    for load in loads[3:]:
        load.wait()

    for copy in share:
        copy.wait_recv()
    total = second[0].astype(F32)
    for j in range(1, far_count):
        total = total + second[j].astype(F32)
    fin[span(near_me)] = total.astype(BF16)
    for copy in gather:
        copy.start()

    for z in range(planes):
        m_left[z].wait_recv()
        m_right[z].wait_recv()
        for t in range(frames):
            total = mown[t, z, half : 2 * half, :]
            total = total + (mown[t - 1, z, 0:half, :] if t > 0 else mrecv[0, z].astype(F32))
            total = total + (mown[t + 1, z, 2 * half : 3 * half, :] if t < frames - 1 else mrecv[1, z].astype(F32))
            rebuilt_ref[t, z] = (y2_ref[t, z].astype(F32) - total).astype(BF16)

    @pl.when(has_l)
    def _():
        for t in range(frames):
            p_right(t).wait_recv()

    @pl.when(jnp.logical_not(has_l))
    def _():
        precv[0] = jnp.zeros_like(precv[0])

    @pl.when(has_r)
    def _():
        for t in range(frames):
            p_left(t).wait_recv()

    @pl.when(jnp.logical_not(has_r))
    def _():
        precv[1] = jnp.zeros_like(precv[1])

    for t in range(frames):
        for z in range(planes):
            total = parts[t, z, half : 2 * half, :]
            total = total + (parts[t, z - 1, 2 * half : 3 * half, :] if z > 0 else precv[0, t].astype(F32))
            total = total + (parts[t, z + 1, 0:half, :] if z < planes - 1 else precv[1, t].astype(F32))
            gin_ref[t, z] = (g1_ref[t, z].astype(F32) + total).astype(BF16)

    for t in range(frames):
        pl.when(has_r)(y_right[t].wait_send)
        pl.when(has_l)(y_left[t].wait_send)
        pl.when(has_r)(p_right(t).wait_send)
        pl.when(has_l)(p_left(t).wait_send)
    for copy in g_left + g_right + m_left + m_right + [copy for _, copy in scatter] + share:
        copy.wait_send()
    for copy in gather:
        copy.wait_recv()
    for copy in gather:
        copy.wait_send()


def finish(factor, rebuilt_in, gin_in, fin, rebuilt_out, gin_out, gs_out, gb_out, gt_out, gs, gb, gt, sem):
    copies = []

    def send(src, dst):
        copies.append(pltpu.make_async_copy(src, dst, sem.at[len(copies)]))
        copies[-1].start()

    send(rebuilt_in, rebuilt_out)
    send(gin_in, gin_out)
    hid, window = gs.shape[1], gs.shape[2]
    half = window // 9
    temporal = sum_layout(half, 1)[0]
    for dz in range(3):
        low, high = dz * window // LANES, -(-(dz + 1) * window // LANES)
        wide = jnp.concatenate([fin[tile].astype(F32) * factor for tile in range(low, high)], axis=1)
        gs[dz] = wide[:, dz * window - low * LANES : (dz + 1) * window - low * LANES]
        send(gs.at[dz], gs_out.at[dz])
    turned = (fin[temporal].astype(F32) * factor).T
    for k in range(3):
        gt[k] = turned[k * half : (k + 1) * half]
    gb[...] = turned[3 * half : 3 * half + 1]
    send(gt, gt_out)
    send(gb, gb_out)
    for copy in copies:
        copy.wait()


def shards(gz_count, ta_count, outputs_fwd, cotangent, spatial_weight, hidden_bias, temporal_weight):
    frames, planes, channels, pix = outputs_fwd.shape
    half = channels // 2
    hid = spatial_weight.shape[1]
    window = 9 * half
    tw = temporal_weight.reshape((3 * half, hid))
    factor = 1.0 / math.sqrt(frames * ta_count * planes * gz_count * ROWS * COLS)
    vmem = pl.BlockSpec(memory_space=pltpu.VMEM)
    hbm = pl.BlockSpec(memory_space=pltpu.HBM)
    near_bits, far_bits = groups_of(gz_count, ta_count)
    near_count, far_count = 1 << len(near_bits), 1 << len(far_bits)
    tiles = sum_layout(half, near_count)[1]
    per = tiles // near_count
    dma = pltpu.SemaphoreType.DMA
    field = jax.ShapeDtypeStruct((frames, planes, half, pix), BF16)
    held = pltpu.VMEM((frames, planes, half, pix), BF16)
    outs = pl.pallas_call(
        functools.partial(kernel, gz_count, ta_count),
        out_shape=(held, held, pltpu.VMEM((tiles, hid, LANES), BF16)),
        in_specs=[hbm] * 5,
        out_specs=(vmem,) * 3,
        scratch_shapes=[
            pltpu.VMEM((frames, (planes + 2) * window, pix), BF16),
            pltpu.VMEM((frames * planes, 9 * hid, pix), BF16),
            pltpu.VMEM((frames, planes, 3 * half, pix), BF16),
            pltpu.VMEM((2, frames, half, pix), BF16),
            pltpu.VMEM((frames, planes, hid, pix), F32),
            pltpu.VMEM((frames, planes, hid, pix), BF16),
            pltpu.VMEM((frames, planes, hid, pix), BF16),
            pltpu.VMEM((frames, planes, 3 * half, pix), F32),
            pltpu.VMEM((frames, planes, 3 * half, pix), F32),
            pltpu.VMEM((2, planes, half, pix), BF16),
            pltpu.VMEM((2, planes, half, pix), BF16),
            pltpu.VMEM((2, frames, half, pix), BF16),
            pltpu.VMEM((2, frames, half, pix), BF16),
            pltpu.VMEM((frames, planes, half, pix), BF16),
            pltpu.VMEM((frames, planes, half, pix), BF16),
            pltpu.VMEM((frames, planes, half, pix), BF16),
            pltpu.VMEM(spatial_weight.shape, BF16),
            pltpu.VMEM((1, hid), F32),
            pltpu.VMEM(tw.shape, BF16),
            pltpu.VMEM((hid, 3 * window), BF16),
            pltpu.VMEM((3 * half, 9 * hid), BF16),
            pltpu.VMEM((tiles, hid, LANES), F32),
            pltpu.VMEM((tiles, hid, LANES), BF16),
            pltpu.VMEM((near_count - 1, per, hid, LANES), BF16),
            pltpu.VMEM((far_count, per, hid, LANES), BF16),
            dma((5,)), dma((frames,)), dma((frames, 3)),
            dma((2, frames)), dma((2, frames)), dma((2, planes)), dma((2, planes)),
            dma((2, planes)), dma((2, planes)), dma((2, frames)), dma((2, frames)),
            dma((near_count - 1,)), dma((near_count - 1,)),
            dma((far_count - 1,)), dma((far_count - 1,)),
            dma((near_count - 1,)), dma((near_count - 1,)),
        ],
        compiler_params=pltpu.CompilerParams(
            collective_id=0, has_side_effects=True, vmem_limit_bytes=60 * 1024 * 1024
        ),
    )(outputs_fwd, cotangent, spatial_weight, hidden_bias[None, :], tw)
    ends = pl.pallas_call(
        functools.partial(finish, factor),
        out_shape=(
            field,
            field,
            jax.ShapeDtypeStruct((3, hid, window), F32),
            jax.ShapeDtypeStruct((1, hid), F32),
            jax.ShapeDtypeStruct((3, half, hid), F32),
        ),
        in_specs=[vmem] * 3,
        out_specs=(hbm,) * 5,
        scratch_shapes=[
            pltpu.VMEM((3, hid, window), F32),
            pltpu.VMEM((1, hid), F32),
            pltpu.VMEM((3, half, hid), F32),
            dma((7,)),
        ],
        compiler_params=pltpu.CompilerParams(vmem_limit_bytes=16 * 1024 * 1024),
    )(*outs)
    return ends[0], ends[1], ends[2], ends[3].reshape((hid,)), ends[4]


def solution(mesh):
    placed = (P("ta", "gz", None, None), P("ta", "gz", None, None), P(), P(), P())
    return jax.shard_map(
        functools.partial(shards, mesh.shape["gz"], mesh.shape["ta"]),
        mesh=mesh,
        in_specs=placed,
        out_specs=(P("ta", "gz", None, None), P("ta", "gz", None, None), P(), P(), P()),
        check_vma=False,
    )
```

```python
import functools
import math

import jax
import jax.numpy as jnp
from jax import lax
from jax.experimental import pallas as pl
from jax.experimental.pallas import tpu as pltpu
from jax.sharding import PartitionSpec as P

ROWS = 8
COLS = 160
LANES = 128
F32 = jnp.float32
BF16 = jnp.bfloat16


def groups_of(gz_count, ta_count):
    bits = lambda count: [1 << i for i in range(count.bit_length() - 1)]
    gz_bits = [("gz", bit) for bit in bits(gz_count)]
    ta_bits = [("ta", bit) for bit in bits(ta_count)]
    return gz_bits[:3], gz_bits[3:] + ta_bits


def sum_layout(half, near_count):
    temporal = -(-27 * half // LANES)
    tiles = temporal + -(-(3 * half + 1) // LANES)
    return temporal, -(-tiles // near_count) * near_count


def nn(lhs, rhs):
    return lax.dot_general(lhs, rhs, (((1,), (0,)), ((), ())), preferred_element_type=F32)


def nt(lhs, rhs):
    return lax.dot_general(lhs, rhs, (((1,), (1,)), ((), ())), preferred_element_type=F32)


def tn(lhs, rhs):
    return lax.dot_general(lhs, rhs, (((0,), (0,)), ((), ())), preferred_element_type=F32)


def kernel(
    gz_count, ta_count,
    x_hbm, g_hbm, sw_hbm, bias_hbm, tw_hbm,
    rebuilt_ref, gin_ref, fin,
    cols, hcols, g3, yh, slope, act, hgr, parts, mown, msend, mrecv, psend, precv,
    y_ref, y2_ref, g1_ref, sw_ref, bias_ref, tw_ref, wcat, flip, acc, accb, first, second,
    lsem, ysem, g3sem,
    ysem_s, ysem_r, gsem_s, gsem_r, msem_s, msem_r, psem_s, psem_r,
    asem_s, asem_r, bsem_s, bsem_r, csem_s, csem_r,
):
    frames, planes, half, pix = y_ref.shape
    hid = bias_ref.shape[1]
    window = 9 * half
    me_g = lax.axis_index("gz")
    me_t = lax.axis_index("ta")
    has_l = me_g > 0
    has_r = me_g < gz_count - 1
    mesh_id = pl.DeviceIdType.MESH
    ta_r = lax.rem(me_t + 1, ta_count)
    ta_l = lax.rem(me_t + ta_count - 1, ta_count)
    near_bits, far_bits = groups_of(gz_count, ta_count)

    def member(group, flip_mask):
        place = {"gz": me_g, "ta": me_t}
        index = 0
        for order, (axis, bit) in enumerate(group):
            at = me_g if axis == "gz" else me_t
            has = lax.rem(at // bit, 2)
            if flip_mask >> order & 1:
                place[axis] = place[axis] + bit - 2 * bit * has
                has = 1 - has
            index = index + (has << order)
        return (place["gz"], place["ta"]), index

    near_count, far_count = 1 << len(near_bits), 1 << len(far_bits)
    barrier = pltpu.get_barrier_semaphore()

    def greet(dev):
        pl.semaphore_signal(barrier, inc=1, device_id=dev, device_id_type=mesh_id)

    greet((me_g, ta_r))
    greet((me_g, ta_l))

    @pl.when(has_l)
    def _():
        greet((me_g - 1, me_t))

    @pl.when(has_r)
    def _():
        greet((me_g + 1, me_t))

    for j in range(1, near_count):
        greet(member(near_bits, j)[0])
    for j in range(1, far_count):
        greet(member(far_bits, j)[0])

    pairs = (
        (sw_hbm, sw_ref), (tw_hbm, tw_ref), (bias_hbm, bias_ref),
        (x_hbm.at[:, :, half : 2 * half], y2_ref), (g_hbm.at[:, :, 0:half], g1_ref),
    )
    loads = [pltpu.make_async_copy(src, dst, lsem.at[i]) for i, (src, dst) in enumerate(pairs)]
    own = [pltpu.make_async_copy(x_hbm.at[t, :, 0:half], y_ref.at[t], ysem.at[t]) for t in range(frames)]
    local = [
        (s, k, pltpu.make_async_copy(
            g_hbm.at[s + 1 - k, :, half : 2 * half], g3.at[s, :, k * half : (k + 1) * half], g3sem.at[s, k]
        ))
        for s in range(frames) for k in range(3) if 0 <= s + 1 - k < frames
    ]
    for load in own + loads[:3]:
        load.start()
    beside = has_l.astype(jnp.int32) + has_r.astype(jnp.int32)
    for load in loads[:3]:
        load.wait()
    for dz in range(3):
        wcat[:, dz * window : (dz + 1) * window] = sw_ref[dz]
        turned = sw_ref[dz].astype(F32).T.astype(BF16)
        for w in range(9):
            flip[dz * half : (dz + 1) * half, w * hid : (w + 1) * hid] = turned[(8 - w) * half : (9 - w) * half]
    bias = jnp.broadcast_to(bias_ref[...], (8, hid)).T[:, 0:1]

    place = lax.broadcasted_iota(jnp.int32, (1, pix), 1)
    column = lax.rem(place, COLS)
    col_ok = {-1: column < COLS - 1, 1: column > 0}
    edge = -(-COLS // LANES) * LANES
    zero = jnp.zeros((), BF16)
    head_ok = place[:, 0:edge] >= COLS
    tail_ok = place[:, pix - edge : pix] < pix - COLS

    def unfold(value, out, base):
        rows = value.shape[0]
        for c in (-1, 0, 1):
            source = value if c == 0 else jnp.where(col_ok[c], value, zero)
            for r in (-1, 0, 1):
                shift = (-(r * COLS + c)) % pix
                moved = pltpu.roll(source, shift, 1) if shift else source
                at = pl.ds(base + (3 * (r + 1) + c + 1) * rows, rows)
                if r == -1:
                    out[at, 0:edge] = jnp.where(head_ok, moved[:, 0:edge], zero)
                    out[at, edge:pix] = moved[:, edge:pix]
                elif r == 1:
                    out[at, 0 : pix - edge] = moved[:, 0 : pix - edge]
                    out[at, pix - edge : pix] = jnp.where(tail_ok, moved[:, pix - edge : pix], zero)
                else:
                    out[at, :] = moved

    for t in range(frames):
        own[t].wait()
        for z in range(planes):
            unfold(y_ref[t, z], cols.at[t], (z + 1) * window)

    pl.semaphore_wait(barrier, near_count + far_count + beside)

    def remote(src, dst, ssem, rsem, dev):
        return pltpu.make_async_remote_copy(
            src_ref=src, dst_ref=dst, send_sem=ssem, recv_sem=rsem, device_id=dev, device_id_type=mesh_id
        )

    y_right = [
        remote(x_hbm.at[t, planes - 1, 0:half], yh.at[0, t], ysem_s.at[0, t], ysem_r.at[0, t], (me_g + 1, me_t))
        for t in range(frames)
    ]
    y_left = [
        remote(x_hbm.at[t, 0, 0:half], yh.at[1, t], ysem_s.at[1, t], ysem_r.at[1, t], (me_g - 1, me_t))
        for t in range(frames)
    ]
    g_left = [
        remote(
            g_hbm.at[0, z, half : 2 * half], g3.at[frames - 1, z, 0:half],
            gsem_s.at[0, z], gsem_r.at[0, z], (me_g, ta_l),
        )
        for z in range(planes)
    ]
    g_right = [
        remote(
            g_hbm.at[frames - 1, z, half : 2 * half], g3.at[0, z, 2 * half : 3 * half],
            gsem_s.at[1, z], gsem_r.at[1, z], (me_g, ta_r),
        )
        for z in range(planes)
    ]
    g_right[0].start()
    for t in range(frames):
        pl.when(has_r)(y_right[t].start)
        pl.when(has_l)(y_left[t].start)
    g_left[0].start()
    for z in range(1, planes):
        g_right[z].start()
        g_left[z].start()
    for _, _, load in local:
        load.start()
    for load in loads[3:]:
        load.start()

    whole = wcat[...]
    tw = tw_ref[...]
    for t in range(frames):
        for z in range(planes):
            lo, hi = max(z, 1), min(z + 3, planes + 1)
            slope[t, z] = nn(whole[:, (lo - z) * window : (hi - z) * window], cols[t, lo * window : hi * window, :]) + bias

    temporal = sum_layout(half, near_count)[0]
    tiles = acc.shape[0]
    per = tiles // near_count

    def span(index):
        return pl.ds(index * per, per)

    near_me = member(near_bits, 0)[1]
    far_me = member(far_bits, 0)[1]
    scatter, share, gather = [], [], []
    for j in reversed(range(1, near_count)):
        dev, index = member(near_bits, j)
        scatter.append((j, remote(accb.at[span(index)], first.at[j - 1], asem_s.at[j - 1], asem_r.at[j - 1], dev)))
        mine = fin.at[span(near_me)]
        gather.append(remote(mine, mine, csem_s.at[j - 1], csem_r.at[j - 1], dev))
    for j in reversed(range(1, far_count)):
        dev, _ = member(far_bits, j)
        share.append(remote(second.at[far_me], second.at[far_me], bsem_s.at[j - 1], bsem_r.at[j - 1], dev))

    back = flip[...]

    def p_right(t):
        return remote(psend.at[0, t], precv.at[0, t], psem_s.at[0, t], psem_r.at[0, t], (me_g + 1, me_t))

    def p_left(t):
        return remote(psend.at[1, t], precv.at[1, t], psem_s.at[1, t], psem_r.at[1, t], (me_g - 1, me_t))

    m_right = [
        remote(msend.at[0, z], mrecv.at[0, z], msem_s.at[0, z], msem_r.at[0, z], (me_g, ta_r)) for z in range(planes)
    ]
    m_left = [
        remote(msend.at[1, z], mrecv.at[1, z], msem_s.at[1, z], msem_r.at[1, z], (me_g, ta_l)) for z in range(planes)
    ]

    def halo(t, side, has, copy):
        base = side * (planes + 1) * window

        @pl.when(has)
        def _():
            copy.wait_recv()
            unfold(yh[side, t], cols.at[t], base)

        @pl.when(jnp.logical_not(has))
        def _():
            cols[t, base : base + window, :] = jnp.zeros((window, pix), BF16)

    def forward(t, z):
        pre = slope[t, z]
        if z == 0:
            pre = pre + nn(whole[:, 0:window], cols[t, 0:window, :])
        if z == planes - 1:
            pre = pre + nn(whole[:, 2 * window : 3 * window], cols[t, (planes + 1) * window : (planes + 2) * window, :])
        sig = jax.nn.sigmoid(pre)
        active = (pre * sig).astype(BF16)
        slope[t, z] = sig * (1.0 + pre * (1.0 - sig))
        act[t, z] = active
        mapped = nn(tw, active)
        mown[t, z] = mapped
        if t == 0:
            msend[1, z] = mapped[2 * half : 3 * half, :].astype(BF16)
            m_left[z].start()
        if t == frames - 1:
            msend[0, z] = mapped[0:half, :].astype(BF16)
            m_right[z].start()

    def sums(t, z, fresh):
        if t == 0:
            g_right[z].wait_recv()
        if t == frames - 1:
            g_left[z].wait_recv()
        around = g3[t, z]
        hgrad = (tn(tw, around) * slope[t, z]).astype(BF16)
        hgr[t, z] = hgrad
        ssum = nt(hgrad, cols[t, z * window : (z + 3) * window, :])
        tsum = nt(act[t, z], around)
        bsum = jnp.sum(hgrad.astype(F32), axis=1, keepdims=True)

        def add(tile, lo, width, value):
            if not fresh:
                value = acc[tile, :, lo : lo + width] + value
            acc[tile, :, lo : lo + width] = value

        for tile in range(temporal):
            width = min(LANES, 3 * window - tile * LANES)
            add(tile, 0, width, ssum[:, tile * LANES : tile * LANES + width])
            if width < LANES and fresh:
                acc[tile, :, width:LANES] = jnp.zeros((hid, LANES - width), F32)
        add(temporal, 0, 3 * half, tsum)
        add(temporal, 3 * half, LANES - 3 * half, jnp.broadcast_to(bsum, (hid, LANES - 3 * half)))

    def adjoint(t, z):
        at = t * planes + z
        unfold(hgr[t, z], hcols.at[at], 0)
        parts[t, z] = nn(back, hcols[at])
        if z == 0:
            psend[1, t] = parts[t, z, 0:half, :].astype(BF16)
        if z == planes - 1:
            psend[0, t] = parts[t, z, 2 * half : 3 * half, :].astype(BF16)

    for t in range(frames):
        halo(t, 0, has_l, y_right[t])
        halo(t, 1, has_r, y_left[t])
        for z in range(planes):
            forward(t, z)
        if t == 0:
            for _, _, load in local:
                load.wait()
        sums(t, 0, t == 0)
    rest = [(t, z) for z in range(1, planes) for t in range(frames)]
    for t, z in rest[:-1]:
        sums(t, z, False)
    done = [(t, 0) for t in range(frames)] + rest
    if rest:
        sums(*rest[-1], False)
    for tile in range(temporal + 1, tiles):
        acc[tile] = jnp.zeros((hid, LANES), F32)
    accb[...] = acc[...].astype(BF16)
    for _, copy in scatter:
        copy.start()
    for t, z in done:
        adjoint(t, z)

    total = acc[span(near_me)]
    for j, copy in scatter:
        copy.wait_recv()
        total = total + first[j - 1].astype(F32)
    second[pl.ds(far_me, 1)] = total.astype(BF16)[None]
    for copy in share:
        copy.start()
    for t in range(frames):
        pl.when(has_l)(p_left(t).start)
        pl.when(has_r)(p_right(t).start)

    for load in loads[3:]:
        load.wait()

    for copy in share:
        copy.wait_recv()
    total = second[0].astype(F32)
    for j in range(1, far_count):
        total = total + second[j].astype(F32)
    fin[span(near_me)] = total.astype(BF16)
    for copy in gather:
        copy.start()

    for z in range(planes):
        m_left[z].wait_recv()
        m_right[z].wait_recv()
        for t in range(frames):
            total = mown[t, z, half : 2 * half, :]
            total = total + (mown[t - 1, z, 0:half, :] if t > 0 else mrecv[0, z].astype(F32))
            total = total + (mown[t + 1, z, 2 * half : 3 * half, :] if t < frames - 1 else mrecv[1, z].astype(F32))
            rebuilt_ref[t, z] = (y2_ref[t, z].astype(F32) - total).astype(BF16)

    @pl.when(has_l)
    def _():
        for t in range(frames):
            p_right(t).wait_recv()

    @pl.when(jnp.logical_not(has_l))
    def _():
        precv[0] = jnp.zeros_like(precv[0])

    @pl.when(has_r)
    def _():
        for t in range(frames):
            p_left(t).wait_recv()

    @pl.when(jnp.logical_not(has_r))
    def _():
        precv[1] = jnp.zeros_like(precv[1])

    for t in range(frames):
        for z in range(planes):
            total = parts[t, z, half : 2 * half, :]
            total = total + (parts[t, z - 1, 2 * half : 3 * half, :] if z > 0 else precv[0, t].astype(F32))
            total = total + (parts[t, z + 1, 0:half, :] if z < planes - 1 else precv[1, t].astype(F32))
            gin_ref[t, z] = (g1_ref[t, z].astype(F32) + total).astype(BF16)

    for t in range(frames):
        pl.when(has_r)(y_right[t].wait_send)
        pl.when(has_l)(y_left[t].wait_send)
        pl.when(has_r)(p_right(t).wait_send)
        pl.when(has_l)(p_left(t).wait_send)
    for copy in g_left + g_right + m_left + m_right + [copy for _, copy in scatter] + share:
        copy.wait_send()
    for copy in gather:
        copy.wait_recv()
    for copy in gather:
        copy.wait_send()


def finish(factor, rebuilt_in, gin_in, fin, rebuilt_out, gin_out, gs_out, gb_out, gt_out, gs, gb, gt, sem):
    copies = []

    def send(src, dst):
        copies.append(pltpu.make_async_copy(src, dst, sem.at[len(copies)]))
        copies[-1].start()

    send(rebuilt_in, rebuilt_out)
    send(gin_in, gin_out)
    hid, window = gs.shape[1], gs.shape[2]
    half = window // 9
    temporal = sum_layout(half, 1)[0]
    for dz in range(3):
        low, high = dz * window // LANES, -(-(dz + 1) * window // LANES)
        wide = jnp.concatenate([fin[tile].astype(F32) * factor for tile in range(low, high)], axis=1)
        gs[dz] = wide[:, dz * window - low * LANES : (dz + 1) * window - low * LANES]
        send(gs.at[dz], gs_out.at[dz])
    turned = (fin[temporal].astype(F32) * factor).T
    for k in range(3):
        gt[k] = turned[k * half : (k + 1) * half]
    gb[...] = turned[3 * half : 3 * half + 1]
    send(gt, gt_out)
    send(gb, gb_out)
    for copy in copies:
        copy.wait()


def shards(gz_count, ta_count, outputs_fwd, cotangent, spatial_weight, hidden_bias, temporal_weight):
    frames, planes, channels, pix = outputs_fwd.shape
    half = channels // 2
    hid = spatial_weight.shape[1]
    window = 9 * half
    tw = temporal_weight.reshape((3 * half, hid))
    factor = 1.0 / math.sqrt(frames * ta_count * planes * gz_count * ROWS * COLS)
    vmem = pl.BlockSpec(memory_space=pltpu.VMEM)
    hbm = pl.BlockSpec(memory_space=pltpu.HBM)
    near_bits, far_bits = groups_of(gz_count, ta_count)
    near_count, far_count = 1 << len(near_bits), 1 << len(far_bits)
    tiles = sum_layout(half, near_count)[1]
    per = tiles // near_count
    dma = pltpu.SemaphoreType.DMA
    field = jax.ShapeDtypeStruct((frames, planes, half, pix), BF16)
    held = pltpu.VMEM((frames, planes, half, pix), BF16)
    outs = pl.pallas_call(
        functools.partial(kernel, gz_count, ta_count),
        out_shape=(held, held, pltpu.VMEM((tiles, hid, LANES), BF16)),
        in_specs=[hbm] * 5,
        out_specs=(vmem,) * 3,
        scratch_shapes=[
            pltpu.VMEM((frames, (planes + 2) * window, pix), BF16),
            pltpu.VMEM((frames * planes, 9 * hid, pix), BF16),
            pltpu.VMEM((frames, planes, 3 * half, pix), BF16),
            pltpu.VMEM((2, frames, half, pix), BF16),
            pltpu.VMEM((frames, planes, hid, pix), F32),
            pltpu.VMEM((frames, planes, hid, pix), BF16),
            pltpu.VMEM((frames, planes, hid, pix), BF16),
            pltpu.VMEM((frames, planes, 3 * half, pix), F32),
            pltpu.VMEM((frames, planes, 3 * half, pix), F32),
            pltpu.VMEM((2, planes, half, pix), BF16),
            pltpu.VMEM((2, planes, half, pix), BF16),
            pltpu.VMEM((2, frames, half, pix), BF16),
            pltpu.VMEM((2, frames, half, pix), BF16),
            pltpu.VMEM((frames, planes, half, pix), BF16),
            pltpu.VMEM((frames, planes, half, pix), BF16),
            pltpu.VMEM((frames, planes, half, pix), BF16),
            pltpu.VMEM(spatial_weight.shape, BF16),
            pltpu.VMEM((1, hid), F32),
            pltpu.VMEM(tw.shape, BF16),
            pltpu.VMEM((hid, 3 * window), BF16),
            pltpu.VMEM((3 * half, 9 * hid), BF16),
            pltpu.VMEM((tiles, hid, LANES), F32),
            pltpu.VMEM((tiles, hid, LANES), BF16),
            pltpu.VMEM((near_count - 1, per, hid, LANES), BF16),
            pltpu.VMEM((far_count, per, hid, LANES), BF16),
            dma((5,)), dma((frames,)), dma((frames, 3)),
            dma((2, frames)), dma((2, frames)), dma((2, planes)), dma((2, planes)),
            dma((2, planes)), dma((2, planes)), dma((2, frames)), dma((2, frames)),
            dma((near_count - 1,)), dma((near_count - 1,)),
            dma((far_count - 1,)), dma((far_count - 1,)),
            dma((near_count - 1,)), dma((near_count - 1,)),
        ],
        compiler_params=pltpu.CompilerParams(
            collective_id=0, has_side_effects=True, vmem_limit_bytes=60 * 1024 * 1024
        ),
    )(outputs_fwd, cotangent, spatial_weight, hidden_bias[None, :], tw)
    ends = pl.pallas_call(
        functools.partial(finish, factor),
        out_shape=(
            field,
            field,
            jax.ShapeDtypeStruct((3, hid, window), F32),
            jax.ShapeDtypeStruct((1, hid), F32),
            jax.ShapeDtypeStruct((3, half, hid), F32),
        ),
        in_specs=[vmem] * 3,
        out_specs=(hbm,) * 5,
        scratch_shapes=[
            pltpu.VMEM((3, hid, window), F32),
            pltpu.VMEM((1, hid), F32),
            pltpu.VMEM((3, half, hid), F32),
            dma((7,)),
        ],
        compiler_params=pltpu.CompilerParams(vmem_limit_bytes=16 * 1024 * 1024),
    )(*outs)
    return ends[0], ends[1], ends[2], ends[3].reshape((hid,)), ends[4]


def solution(mesh):
    placed = (P("ta", "gz", None, None), P("ta", "gz", None, None), P(), P(), P())
    return jax.shard_map(
        functools.partial(shards, mesh.shape["gz"], mesh.shape["ta"]),
        mesh=mesh,
        in_specs=placed,
        out_specs=(P("ta", "gz", None, None), P("ta", "gz", None, None), P(), P(), P()),
        check_vma=False,
    )
```

```python
import functools
import math

import jax
import jax.numpy as jnp
from jax import lax
from jax.experimental import pallas as pl
from jax.experimental.pallas import tpu as pltpu
from jax.sharding import PartitionSpec as P

ROWS = 8
COLS = 160
LANES = 128
F32 = jnp.float32
BF16 = jnp.bfloat16


def groups_of(gz_count, ta_count):
    bits = lambda count: [1 << i for i in range(count.bit_length() - 1)]
    gz_bits = [("gz", bit) for bit in bits(gz_count)]
    ta_bits = [("ta", bit) for bit in bits(ta_count)]
    return gz_bits[:3], gz_bits[3:] + ta_bits


def sum_layout(half, near_count):
    temporal = -(-27 * half // LANES)
    tiles = temporal + -(-(3 * half + 1) // LANES)
    return temporal, -(-tiles // near_count) * near_count


def nn(lhs, rhs):
    return lax.dot_general(lhs, rhs, (((1,), (0,)), ((), ())), preferred_element_type=F32)


def nt(lhs, rhs):
    return lax.dot_general(lhs, rhs, (((1,), (1,)), ((), ())), preferred_element_type=F32)


def tn(lhs, rhs):
    return lax.dot_general(lhs, rhs, (((0,), (0,)), ((), ())), preferred_element_type=F32)


def kernel(
    gz_count, ta_count,
    x_hbm, g_hbm, sw_hbm, bias_hbm, tw_hbm,
    rebuilt_ref, gin_ref, fin,
    cols, hcols, g3, yh, slope, act, hgr, parts, mown, msend, mrecv, psend, precv,
    y_ref, y2_ref, g1_ref, sw_ref, bias_ref, tw_ref, wcat, flip, acc, accb, first, second,
    lsem, ysem, g3sem,
    ysem_s, ysem_r, gsem_s, gsem_r, msem_s, msem_r, psem_s, psem_r,
    asem_s, asem_r, bsem_s, bsem_r, csem_s, csem_r,
):
    frames, planes, half, pix = y_ref.shape
    hid = bias_ref.shape[1]
    window = 9 * half
    me_g = lax.axis_index("gz")
    me_t = lax.axis_index("ta")
    has_l = me_g > 0
    has_r = me_g < gz_count - 1
    mesh_id = pl.DeviceIdType.MESH
    ta_r = lax.rem(me_t + 1, ta_count)
    ta_l = lax.rem(me_t + ta_count - 1, ta_count)
    near_bits, far_bits = groups_of(gz_count, ta_count)

    def member(group, flip_mask):
        place = {"gz": me_g, "ta": me_t}
        index = 0
        for order, (axis, bit) in enumerate(group):
            at = me_g if axis == "gz" else me_t
            has = lax.rem(at // bit, 2)
            if flip_mask >> order & 1:
                place[axis] = place[axis] + bit - 2 * bit * has
                has = 1 - has
            index = index + (has << order)
        return (place["gz"], place["ta"]), index

    near_count, far_count = 1 << len(near_bits), 1 << len(far_bits)
    barrier = pltpu.get_barrier_semaphore()

    def greet(dev):
        pl.semaphore_signal(barrier, inc=1, device_id=dev, device_id_type=mesh_id)

    greet((me_g, ta_r))
    greet((me_g, ta_l))

    @pl.when(has_l)
    def _():
        greet((me_g - 1, me_t))

    @pl.when(has_r)
    def _():
        greet((me_g + 1, me_t))

    for j in range(1, near_count):
        greet(member(near_bits, j)[0])
    for j in range(1, far_count):
        greet(member(far_bits, j)[0])

    pairs = (
        (sw_hbm, sw_ref), (tw_hbm, tw_ref), (bias_hbm, bias_ref),
        (x_hbm.at[:, :, half : 2 * half], y2_ref), (g_hbm.at[:, :, 0:half], g1_ref),
    )
    loads = [pltpu.make_async_copy(src, dst, lsem.at[i]) for i, (src, dst) in enumerate(pairs)]
    own = [pltpu.make_async_copy(x_hbm.at[t, :, 0:half], y_ref.at[t], ysem.at[t]) for t in range(frames)]
    local = [
        (s, k, pltpu.make_async_copy(
            g_hbm.at[s + 1 - k, :, half : 2 * half], g3.at[s, :, k * half : (k + 1) * half], g3sem.at[s, k]
        ))
        for s in range(frames) for k in range(3) if 0 <= s + 1 - k < frames
    ]
    for load in own + loads[:3]:
        load.start()
    beside = has_l.astype(jnp.int32) + has_r.astype(jnp.int32)
    for load in loads[:3]:
        load.wait()
    for dz in range(3):
        wcat[:, dz * window : (dz + 1) * window] = sw_ref[dz]
        turned = sw_ref[dz].astype(F32).T.astype(BF16)
        for w in range(9):
            flip[dz * half : (dz + 1) * half, w * hid : (w + 1) * hid] = turned[(8 - w) * half : (9 - w) * half]
    bias = jnp.broadcast_to(bias_ref[...], (8, hid)).T[:, 0:1]

    place = lax.broadcasted_iota(jnp.int32, (1, pix), 1)
    column = lax.rem(place, COLS)
    col_ok = {-1: column < COLS - 1, 1: column > 0}
    edge = -(-COLS // LANES) * LANES
    zero = jnp.zeros((), BF16)
    head_ok = place[:, 0:edge] >= COLS
    tail_ok = place[:, pix - edge : pix] < pix - COLS

    def unfold(value, out, base):
        rows = value.shape[0]
        for c in (-1, 0, 1):
            source = value if c == 0 else jnp.where(col_ok[c], value, zero)
            for r in (-1, 0, 1):
                shift = (-(r * COLS + c)) % pix
                moved = pltpu.roll(source, shift, 1) if shift else source
                at = pl.ds(base + (3 * (r + 1) + c + 1) * rows, rows)
                if r == -1:
                    out[at, 0:edge] = jnp.where(head_ok, moved[:, 0:edge], zero)
                    out[at, edge:pix] = moved[:, edge:pix]
                elif r == 1:
                    out[at, 0 : pix - edge] = moved[:, 0 : pix - edge]
                    out[at, pix - edge : pix] = jnp.where(tail_ok, moved[:, pix - edge : pix], zero)
                else:
                    out[at, :] = moved

    for t in range(frames):
        own[t].wait()
        for z in range(planes):
            unfold(y_ref[t, z], cols.at[t], (z + 1) * window)

    pl.semaphore_wait(barrier, near_count + far_count + beside)

    def remote(src, dst, ssem, rsem, dev):
        return pltpu.make_async_remote_copy(
            src_ref=src, dst_ref=dst, send_sem=ssem, recv_sem=rsem, device_id=dev, device_id_type=mesh_id
        )

    y_right = [
        remote(x_hbm.at[t, planes - 1, 0:half], yh.at[0, t], ysem_s.at[0, t], ysem_r.at[0, t], (me_g + 1, me_t))
        for t in range(frames)
    ]
    y_left = [
        remote(x_hbm.at[t, 0, 0:half], yh.at[1, t], ysem_s.at[1, t], ysem_r.at[1, t], (me_g - 1, me_t))
        for t in range(frames)
    ]
    g_left = [
        remote(
            g_hbm.at[0, z, half : 2 * half], g3.at[frames - 1, z, 0:half],
            gsem_s.at[0, z], gsem_r.at[0, z], (me_g, ta_l),
        )
        for z in range(planes)
    ]
    g_right = [
        remote(
            g_hbm.at[frames - 1, z, half : 2 * half], g3.at[0, z, 2 * half : 3 * half],
            gsem_s.at[1, z], gsem_r.at[1, z], (me_g, ta_r),
        )
        for z in range(planes)
    ]
    g_right[0].start()
    for t in range(frames):
        pl.when(has_r)(y_right[t].start)
        pl.when(has_l)(y_left[t].start)
    for copy in g_right[1:] + g_left:
        copy.start()
    for _, _, load in local:
        load.start()
    for load in loads[3:]:
        load.start()

    whole = wcat[...]
    tw = tw_ref[...]
    for t in range(frames):
        for z in range(planes):
            lo, hi = max(z, 1), min(z + 3, planes + 1)
            slope[t, z] = nn(whole[:, (lo - z) * window : (hi - z) * window], cols[t, lo * window : hi * window, :]) + bias

    temporal = sum_layout(half, near_count)[0]
    tiles = acc.shape[0]
    per = tiles // near_count

    def span(index):
        return pl.ds(index * per, per)

    near_me = member(near_bits, 0)[1]
    far_me = member(far_bits, 0)[1]
    scatter, share, gather = [], [], []
    for j in reversed(range(1, near_count)):
        dev, index = member(near_bits, j)
        scatter.append((j, remote(accb.at[span(index)], first.at[j - 1], asem_s.at[j - 1], asem_r.at[j - 1], dev)))
        mine = fin.at[span(near_me)]
        gather.append(remote(mine, mine, csem_s.at[j - 1], csem_r.at[j - 1], dev))
    for j in reversed(range(1, far_count)):
        dev, _ = member(far_bits, j)
        share.append(remote(second.at[far_me], second.at[far_me], bsem_s.at[j - 1], bsem_r.at[j - 1], dev))

    back = flip[...]

    def p_right(t):
        return remote(psend.at[0, t], precv.at[0, t], psem_s.at[0, t], psem_r.at[0, t], (me_g + 1, me_t))

    def p_left(t):
        return remote(psend.at[1, t], precv.at[1, t], psem_s.at[1, t], psem_r.at[1, t], (me_g - 1, me_t))

    m_right = [
        remote(msend.at[0, z], mrecv.at[0, z], msem_s.at[0, z], msem_r.at[0, z], (me_g, ta_r)) for z in range(planes)
    ]
    m_left = [
        remote(msend.at[1, z], mrecv.at[1, z], msem_s.at[1, z], msem_r.at[1, z], (me_g, ta_l)) for z in range(planes)
    ]

    def halo(t, side, has, copy):
        base = side * (planes + 1) * window

        @pl.when(has)
        def _():
            copy.wait_recv()
            unfold(yh[side, t], cols.at[t], base)

        @pl.when(jnp.logical_not(has))
        def _():
            cols[t, base : base + window, :] = jnp.zeros((window, pix), BF16)

    def forward(t, z):
        pre = slope[t, z]
        if z == 0:
            pre = pre + nn(whole[:, 0:window], cols[t, 0:window, :])
        if z == planes - 1:
            pre = pre + nn(whole[:, 2 * window : 3 * window], cols[t, (planes + 1) * window : (planes + 2) * window, :])
        sig = jax.nn.sigmoid(pre)
        active = (pre * sig).astype(BF16)
        slope[t, z] = sig * (1.0 + pre * (1.0 - sig))
        act[t, z] = active
        mapped = nn(tw, active)
        mown[t, z] = mapped
        if t == 0:
            msend[1, z] = mapped[2 * half : 3 * half, :].astype(BF16)
            m_left[z].start()
        if t == frames - 1:
            msend[0, z] = mapped[0:half, :].astype(BF16)

    def sums(t, z, fresh):
        if t == 0:
            g_right[z].wait_recv()
        if t == frames - 1:
            g_left[z].wait_recv()
        around = g3[t, z]
        hgrad = (tn(tw, around) * slope[t, z]).astype(BF16)
        hgr[t, z] = hgrad
        ssum = nt(hgrad, cols[t, z * window : (z + 3) * window, :])
        tsum = nt(act[t, z], around)
        bsum = jnp.sum(hgrad.astype(F32), axis=1, keepdims=True)

        def add(tile, lo, width, value):
            if not fresh:
                value = acc[tile, :, lo : lo + width] + value
            acc[tile, :, lo : lo + width] = value

        for tile in range(temporal):
            width = min(LANES, 3 * window - tile * LANES)
            add(tile, 0, width, ssum[:, tile * LANES : tile * LANES + width])
            if width < LANES and fresh:
                acc[tile, :, width:LANES] = jnp.zeros((hid, LANES - width), F32)
        add(temporal, 0, 3 * half, tsum)
        add(temporal, 3 * half, LANES - 3 * half, jnp.broadcast_to(bsum, (hid, LANES - 3 * half)))

    def adjoint(t, z):
        at = t * planes + z
        unfold(hgr[t, z], hcols.at[at], 0)
        parts[t, z] = nn(back, hcols[at])
        if z == 0:
            psend[1, t] = parts[t, z, 0:half, :].astype(BF16)
        if z == planes - 1:
            psend[0, t] = parts[t, z, 2 * half : 3 * half, :].astype(BF16)

    for t in range(frames):
        halo(t, 0, has_l, y_right[t])
        halo(t, 1, has_r, y_left[t])
        for z in range(planes):
            forward(t, z)
        if t == 0:
            for _, _, load in local:
                load.wait()
        for z in range(planes):
            sums(t, z, t == 0 and z == 0)
    done = [(t, z) for z in range(planes) for t in range(frames)]
    for tile in range(temporal + 1, tiles):
        acc[tile] = jnp.zeros((hid, LANES), F32)
    accb[...] = acc[...].astype(BF16)
    for _, copy in scatter:
        copy.start()
    for t, z in done:
        adjoint(t, z)

    total = acc[span(near_me)]
    for j, copy in scatter:
        copy.wait_recv()
        total = total + first[j - 1].astype(F32)
    second[pl.ds(far_me, 1)] = total.astype(BF16)[None]
    for copy in share:
        copy.start()
    for copy in m_right:
        copy.start()
    for t in range(frames):
        pl.when(has_l)(p_left(t).start)
        pl.when(has_r)(p_right(t).start)

    for load in loads[3:]:
        load.wait()

    for copy in share:
        copy.wait_recv()
    total = second[0].astype(F32)
    for j in range(1, far_count):
        total = total + second[j].astype(F32)
    fin[span(near_me)] = total.astype(BF16)
    for copy in gather:
        copy.start()

    for z in range(planes):
        m_left[z].wait_recv()
        m_right[z].wait_recv()
        for t in range(frames):
            total = mown[t, z, half : 2 * half, :]
            total = total + (mown[t - 1, z, 0:half, :] if t > 0 else mrecv[0, z].astype(F32))
            total = total + (mown[t + 1, z, 2 * half : 3 * half, :] if t < frames - 1 else mrecv[1, z].astype(F32))
            rebuilt_ref[t, z] = (y2_ref[t, z].astype(F32) - total).astype(BF16)

    @pl.when(has_l)
    def _():
        for t in range(frames):
            p_right(t).wait_recv()

    @pl.when(jnp.logical_not(has_l))
    def _():
        precv[0] = jnp.zeros_like(precv[0])

    @pl.when(has_r)
    def _():
        for t in range(frames):
            p_left(t).wait_recv()

    @pl.when(jnp.logical_not(has_r))
    def _():
        precv[1] = jnp.zeros_like(precv[1])

    for t in range(frames):
        for z in range(planes):
            total = parts[t, z, half : 2 * half, :]
            total = total + (parts[t, z - 1, 2 * half : 3 * half, :] if z > 0 else precv[0, t].astype(F32))
            total = total + (parts[t, z + 1, 0:half, :] if z < planes - 1 else precv[1, t].astype(F32))
            gin_ref[t, z] = (g1_ref[t, z].astype(F32) + total).astype(BF16)

    for t in range(frames):
        pl.when(has_r)(y_right[t].wait_send)
        pl.when(has_l)(y_left[t].wait_send)
        pl.when(has_r)(p_right(t).wait_send)
        pl.when(has_l)(p_left(t).wait_send)
    for copy in g_left + g_right + m_left + m_right + [copy for _, copy in scatter] + share:
        copy.wait_send()
    for copy in gather:
        copy.wait_recv()
    for copy in gather:
        copy.wait_send()


def finish(factor, rebuilt_in, gin_in, fin, rebuilt_out, gin_out, gs_out, gb_out, gt_out, gs, gb, gt, sem):
    copies = []

    def send(src, dst):
        copies.append(pltpu.make_async_copy(src, dst, sem.at[len(copies)]))
        copies[-1].start()

    send(rebuilt_in, rebuilt_out)
    send(gin_in, gin_out)
    hid, window = gs.shape[1], gs.shape[2]
    half = window // 9
    temporal = sum_layout(half, 1)[0]
    for dz in range(3):
        low, high = dz * window // LANES, -(-(dz + 1) * window // LANES)
        wide = jnp.concatenate([fin[tile].astype(F32) * factor for tile in range(low, high)], axis=1)
        gs[dz] = wide[:, dz * window - low * LANES : (dz + 1) * window - low * LANES]
        send(gs.at[dz], gs_out.at[dz])
    turned = (fin[temporal].astype(F32) * factor).T
    for k in range(3):
        gt[k] = turned[k * half : (k + 1) * half]
    gb[...] = turned[3 * half : 3 * half + 1]
    send(gt, gt_out)
    send(gb, gb_out)
    for copy in copies:
        copy.wait()


def shards(gz_count, ta_count, outputs_fwd, cotangent, spatial_weight, hidden_bias, temporal_weight):
    frames, planes, channels, pix = outputs_fwd.shape
    half = channels // 2
    hid = spatial_weight.shape[1]
    window = 9 * half
    tw = temporal_weight.reshape((3 * half, hid))
    factor = 1.0 / math.sqrt(frames * ta_count * planes * gz_count * ROWS * COLS)
    vmem = pl.BlockSpec(memory_space=pltpu.VMEM)
    hbm = pl.BlockSpec(memory_space=pltpu.HBM)
    near_bits, far_bits = groups_of(gz_count, ta_count)
    near_count, far_count = 1 << len(near_bits), 1 << len(far_bits)
    tiles = sum_layout(half, near_count)[1]
    per = tiles // near_count
    dma = pltpu.SemaphoreType.DMA
    field = jax.ShapeDtypeStruct((frames, planes, half, pix), BF16)
    held = pltpu.VMEM((frames, planes, half, pix), BF16)
    outs = pl.pallas_call(
        functools.partial(kernel, gz_count, ta_count),
        out_shape=(held, held, pltpu.VMEM((tiles, hid, LANES), BF16)),
        in_specs=[hbm] * 5,
        out_specs=(vmem,) * 3,
        scratch_shapes=[
            pltpu.VMEM((frames, (planes + 2) * window, pix), BF16),
            pltpu.VMEM((frames * planes, 9 * hid, pix), BF16),
            pltpu.VMEM((frames, planes, 3 * half, pix), BF16),
            pltpu.VMEM((2, frames, half, pix), BF16),
            pltpu.VMEM((frames, planes, hid, pix), F32),
            pltpu.VMEM((frames, planes, hid, pix), BF16),
            pltpu.VMEM((frames, planes, hid, pix), BF16),
            pltpu.VMEM((frames, planes, 3 * half, pix), F32),
            pltpu.VMEM((frames, planes, 3 * half, pix), F32),
            pltpu.VMEM((2, planes, half, pix), BF16),
            pltpu.VMEM((2, planes, half, pix), BF16),
            pltpu.VMEM((2, frames, half, pix), BF16),
            pltpu.VMEM((2, frames, half, pix), BF16),
            pltpu.VMEM((frames, planes, half, pix), BF16),
            pltpu.VMEM((frames, planes, half, pix), BF16),
            pltpu.VMEM((frames, planes, half, pix), BF16),
            pltpu.VMEM(spatial_weight.shape, BF16),
            pltpu.VMEM((1, hid), F32),
            pltpu.VMEM(tw.shape, BF16),
            pltpu.VMEM((hid, 3 * window), BF16),
            pltpu.VMEM((3 * half, 9 * hid), BF16),
            pltpu.VMEM((tiles, hid, LANES), F32),
            pltpu.VMEM((tiles, hid, LANES), BF16),
            pltpu.VMEM((near_count - 1, per, hid, LANES), BF16),
            pltpu.VMEM((far_count, per, hid, LANES), BF16),
            dma((5,)), dma((frames,)), dma((frames, 3)),
            dma((2, frames)), dma((2, frames)), dma((2, planes)), dma((2, planes)),
            dma((2, planes)), dma((2, planes)), dma((2, frames)), dma((2, frames)),
            dma((near_count - 1,)), dma((near_count - 1,)),
            dma((far_count - 1,)), dma((far_count - 1,)),
            dma((near_count - 1,)), dma((near_count - 1,)),
        ],
        compiler_params=pltpu.CompilerParams(
            collective_id=0, has_side_effects=True, vmem_limit_bytes=60 * 1024 * 1024
        ),
    )(outputs_fwd, cotangent, spatial_weight, hidden_bias[None, :], tw)
    ends = pl.pallas_call(
        functools.partial(finish, factor),
        out_shape=(
            field,
            field,
            jax.ShapeDtypeStruct((3, hid, window), F32),
            jax.ShapeDtypeStruct((1, hid), F32),
            jax.ShapeDtypeStruct((3, half, hid), F32),
        ),
        in_specs=[vmem] * 3,
        out_specs=(hbm,) * 5,
        scratch_shapes=[
            pltpu.VMEM((3, hid, window), F32),
            pltpu.VMEM((1, hid), F32),
            pltpu.VMEM((3, half, hid), F32),
            dma((7,)),
        ],
        compiler_params=pltpu.CompilerParams(vmem_limit_bytes=16 * 1024 * 1024),
    )(*outs)
    return ends[0], ends[1], ends[2], ends[3].reshape((hid,)), ends[4]


def solution(mesh):
    placed = (P("ta", "gz", None, None), P("ta", "gz", None, None), P(), P(), P())
    return jax.shard_map(
        functools.partial(shards, mesh.shape["gz"], mesh.shape["ta"]),
        mesh=mesh,
        in_specs=placed,
        out_specs=(P("ta", "gz", None, None), P("ta", "gz", None, None), P(), P(), P()),
        check_vma=False,
    )
```
